32 devices in a mesh: seq: 16 (over z, y, x), span: 2 (over core).
Axes of the slice: x: 2, y: 2, z: 4, core: 2. Of those that a mesh axis runs over, the one named last changes fastest.
Arguments:
- query: bfloat16 [2, 2048, 3072], P('span', 'seq'), may hold values from -180 to 180
- dout: bfloat16 [2, 2048, 3072], P('span', 'seq'), may hold values from -16 to 16
- mem_key: bfloat16 [2, 768, 3072], P('span', 'seq'), may hold values from -7 to 7
- mem_value: bfloat16 [2, 768, 3072], P('span', 'seq'), may hold values from -6 to 6
- keep_count: int32 [2, 16], P('span'), may hold values from 1 to 48, 256 in all within a row
- keep_slot: int32 [2, 768, 4], P('span', 'seq'), may hold values from 0 to 127
- pool_weight: float32 [2, 768, 4], P('span', 'seq'), may hold values from 0.5 to 1.5
Outputs:
- dquery: bfloat16 [2, 2048, 3072], P('span', 'seq')
- dkey_tok: bfloat16 [2, 2048, 3072], P('span', 'seq')
- dvalue_tok: bfloat16 [2, 2048, 3072], P('span', 'seq')
The draws below stay inside these ranges and needn't reach their ends.
Inputs may be any that keep to these rules, and one draw needn't show every extreme that they name: `keep_count`: each span's counts sum to 256, and the largest is 48.
All inputs are finite; a program needn't handle non-finite values.
Results may differ from the reference program's by a relative error of at most 0.011.
Values may be sent and summed in bfloat16 or wider, within the bound.
A program may use at most 64 MiB of HBM per device.

```python
import math
import jax
import jax.numpy as jnp
import numpy as np
from jax import lax

HEADS = 24
HEAD_DIM = 128
POOL = 4
TOK_DEV = 128
MEM = 256
WIDTH = 3072
TOKENS = 2048
SPANS = 2
OWNERS = 16
CAP = 48
SLOTS = 768


def joint_draw(key):
    key_query, key_memory = jax.random.split(jax.random.fold_in(key, 11), 2)
    query_raw = jnp.clip(jax.random.normal(key_query, (SPANS, TOKENS, WIDTH), jnp.float32), -6.0, 6.0)
    memory_raw = jnp.clip(jax.random.normal(key_memory, (SPANS, SLOTS, WIDTH), jnp.float32), -6.0, 6.0)
    return (query_raw, memory_raw)


def draw_query(key, part):
    return joint_draw(key)[0].astype(jnp.bfloat16)


def draw_mem_key(key, part):
    return joint_draw(key)[1].astype(jnp.bfloat16)


def with_ends(entries, rng, smallest, top_value):
    longest = entries.shape.index(max(entries.shape))
    spots = []
    for shift in (0, 1):
        where = [jax.random.randint(jax.random.fold_in(rng, axis), (), 0, length) for axis, length in enumerate(entries.shape)]
        where[longest] = (where[longest] + shift) % entries.shape[longest]
        spots.append(tuple(where))
    return entries.at[spots[0]].set(smallest).at[spots[1]].set(top_value)


def level_of(key, dims, cuts, smallest, high):
    loudness = 1.0
    for position, shards_of in cuts:
        draws = jax.random.uniform(jax.random.fold_in(jax.random.fold_in(key, 6), position), (shards_of,), jnp.float32, smallest / len(cuts), high / len(cuts))
        loudness = loudness * jnp.repeat(jnp.exp(draws), dims[position] // shards_of).reshape((-1,) + (1,) * (len(dims) - 1 - position))
    return loudness


def profile(number_of, total, bound, slope):
    loads = [(1 << 20) // math.isqrt(standing ** slope) + 1 for standing in range(2, number_of + 1)]
    surplus, counts = total - bound - (number_of - 1), [1] * (number_of - 1)
    while surplus > 0:
        movable = [i for i in range(number_of - 1) if counts[i] < bound]
        pool, remaining = sum([loads[i] for i in movable]), surplus
        for i in movable:
            more = min(bound - counts[i], max(1, remaining * loads[i] // pool), surplus)
            counts[i] = counts[i] + more
            surplus = surplus - more
    return np.array([bound] + counts)


def ragged_sizes(stream_key, count, total, limit, skew):
    if count == 2:
        one = jax.random.randint(stream_key, (), max(1, total - limit), min(limit, total - 1) + 1)
        return jnp.stack([one, total - one])
    sizes = jnp.asarray(profile(count, total, limit, skew), jnp.int32)
    pairs = (count - 1) // 2
    donor, receiver = sizes[1:1 + 2 * pairs:2], sizes[2:2 + 2 * pairs:2]
    margin = jnp.minimum(donor - 1, limit - receiver)
    moved = jax.random.randint(jax.random.fold_in(stream_key, 1), (pairs,), 0, 1 << 20) % (margin + 1)
    sizes = sizes.at[1:1 + 2 * pairs:2].set(donor - moved).at[2:2 + 2 * pairs:2].set(receiver + moved)
    return sizes[jax.random.permutation(jax.random.fold_in(stream_key, 2), count)]


def scatter_about(rng, shape, width, bound, shards=(), kind=jnp.bfloat16):
    loudness = level_of(rng, shape, shards, -0.22, 0.18) if shards else 1.0
    entries = jax.random.normal(rng, shape, jnp.float32) * width * loudness
    return jnp.minimum(jnp.maximum(entries, -bound), bound).astype(kind)


def setup_inputs(seed: int = 0) -> dict:
    arg_keys = jax.random.split(jax.random.key(seed), 8)
    query = draw_query(jax.random.fold_in(arg_keys[7], 71), 0)
    dout = scatter_about(arg_keys[1], (SPANS, TOKENS, WIDTH), 4.0, 16.0, ((0, 2), (1, 16)))
    mem_key = draw_mem_key(jax.random.fold_in(arg_keys[7], 71), 0)
    mem_value = scatter_about(arg_keys[3], (SPANS, SLOTS, WIDTH), 1.0, 6.0, ((0, 2), (1, 16)))
    keep_count = jax.vmap(lambda own: ragged_sizes(own, OWNERS, MEM, CAP, 2))(jax.random.split(arg_keys[4], SPANS)).reshape((SPANS, OWNERS)).astype(jnp.int32)
    keep_slot = with_ends(jax.random.randint(arg_keys[5], (SPANS, SLOTS, POOL), 0, TOK_DEV), jax.random.fold_in(arg_keys[5], 1), 0, TOK_DEV - 1).astype(jnp.int32)
    pool_weight = jnp.clip(0.5 + 1.0 * jax.random.uniform(arg_keys[6], (SPANS, SLOTS, POOL), jnp.float32) ** level_of(arg_keys[6], (SPANS, SLOTS, POOL), ((0, 2), (1, 16)), -0.2, 0.2), 0.5, 1.5)
    return {"query": query, "dout": dout, "mem_key": mem_key, "mem_value": mem_value, "keep_count": keep_count, "keep_slot": keep_slot, "pool_weight": pool_weight}


def full_backward(query_head, grad_head, key_head, value_head, live_mask):
    score_scale = HEAD_DIM ** -0.5
    scores = jnp.dot(query_head, key_head.T, preferred_element_type=jnp.float32) * score_scale
    scores = jnp.where(live_mask[None, :], scores, -jnp.inf)
    shifted = jnp.exp(scores - jnp.max(scores, axis=1, keepdims=True))
    probs_full = shifted / jnp.sum(shifted, axis=1, keepdims=True)
    probs_low = probs_full.astype(jnp.bfloat16)
    attn_out = jnp.dot(probs_low, value_head, preferred_element_type=jnp.float32)
    deltas = jnp.sum(grad_head.astype(jnp.float32) * attn_out, axis=1, keepdims=True)
    probs_grad = jnp.dot(grad_head, value_head.T, preferred_element_type=jnp.float32)
    scores_grad = (probs_full * (probs_grad - deltas)).astype(jnp.bfloat16)
    query_grad = (jnp.dot(scores_grad, key_head, preferred_element_type=jnp.float32) * score_scale).astype(jnp.bfloat16)
    key_grad = jnp.dot(scores_grad.T, query_head, preferred_element_type=jnp.float32) * score_scale
    value_grad = jnp.dot(probs_low.T, grad_head, preferred_element_type=jnp.float32)
    return query_grad, key_grad, value_grad


def split_heads(values, length):
    return jnp.moveaxis(values.reshape(length, HEADS, HEAD_DIM), 1, 0)


def reference(query, dout, mem_key, mem_value, keep_count, keep_slot, pool_weight):
    query_grads = []
    pooled = []
    for span_index in range(SPANS):
        live_mask = (jnp.arange(SLOTS) % CAP) < jnp.repeat(keep_count[span_index], CAP)

        def one_head(pieces):
            return full_backward(pieces[0], pieces[1], pieces[2], pieces[3], live_mask)

        head_query, head_key, head_value = lax.map(one_head, (split_heads(query[span_index], TOKENS), split_heads(dout[span_index], TOKENS), split_heads(mem_key[span_index], SLOTS), split_heads(mem_value[span_index], SLOTS)))
        query_grads.append(jnp.moveaxis(head_query, 0, 1).reshape(TOKENS, WIDTH))
        key_grad = jnp.moveaxis(head_key, 0, 1).reshape(SLOTS, WIDTH)
        value_grad = jnp.moveaxis(head_value, 0, 1).reshape(SLOTS, WIDTH)
        positions = jnp.arange(TOK_DEV).astype(jnp.int32)
        onehot = (keep_slot[span_index].reshape(OWNERS, CAP, POOL)[..., None] == positions).astype(jnp.float32)
        matrix = jnp.einsum("scjt,scj->stc", onehot, pool_weight[span_index].reshape(OWNERS, CAP, POOL), precision=lax.Precision.HIGHEST)
        stacked = jnp.concatenate([key_grad, value_grad], axis=1).reshape(OWNERS, CAP, 2 * WIDTH)
        tokens_grad = jnp.einsum("stc,scw->stw", matrix, stacked, precision=lax.Precision.HIGHEST)
        pooled.append(tokens_grad.reshape(TOKENS, 2 * WIDTH))
    zero_rows = jnp.zeros((TOKENS, 2 * WIDTH), jnp.float32)
    handed = jnp.stack(pooled[1:] + [zero_rows]).astype(jnp.bfloat16)
    return jnp.stack(query_grads), handed[:, :, :WIDTH], handed[:, :, WIDTH:]
```

```python
import math

import jax
import jax.numpy as jnp
from jax import lax
from jax.experimental import pallas as pl
from jax.experimental.pallas import tpu as pltpu
from jax.sharding import PartitionSpec as P

HEAD_DIM = 128
LIVE = 256
BF = jnp.bfloat16
F32 = jnp.float32


def passed_along(block, axis, distance):
    devices = range(lax.axis_size(axis))
    route = [(i - distance, i) for i in devices if i - distance in devices]
    return lax.ppermute(block, axis, route)


def head_backward(query_head, grad_head, key_head, value_head, live_mask, block_rows):
    score_scale = key_head.shape[1] ** (-0.5)
    head_width = query_head.shape[1]
    blocks = query_head.shape[0] // block_rows
    query_blocks = query_head.reshape(blocks, block_rows, head_width)
    grad_blocks = grad_head.reshape(blocks, block_rows, head_width)

    def visit_block(totals, inputs):
        key_grad, value_grad = totals
        query_block, grad_block = inputs
        scores = jnp.dot(query_block, key_head.T, preferred_element_type=jnp.float32) * score_scale
        scores = jnp.where(live_mask[None, :], scores, -jnp.inf)
        shifted = jnp.exp(scores - jnp.max(scores, axis=1, keepdims=True))
        probs_full = shifted / jnp.sum(shifted, axis=1, keepdims=True)
        probs_low = probs_full.astype(jnp.bfloat16)
        attn_out = jnp.dot(probs_low, value_head, preferred_element_type=jnp.float32)
        deltas = jnp.sum(grad_block.astype(jnp.float32) * attn_out, axis=1, keepdims=True)
        probs_grad = jnp.dot(grad_block, value_head.T, preferred_element_type=jnp.float32)
        scores_grad = (probs_full * (probs_grad - deltas)).astype(jnp.bfloat16)
        query_grad = (
            jnp.dot(scores_grad, key_head, preferred_element_type=jnp.float32) * score_scale
        ).astype(jnp.bfloat16)
        key_grad = (
            key_grad
            + lax.dot_general(
                scores_grad,
                query_block,
                (((0,), (0,)), ((), ())),
                preferred_element_type=jnp.float32,
            )
            * score_scale
        )
        value_grad = value_grad + lax.dot_general(
            probs_low, grad_block, (((0,), (0,)), ((), ())), preferred_element_type=jnp.float32
        )
        return ((key_grad, value_grad), query_grad)

    empty_grad = jnp.zeros(key_head.shape, jnp.float32)
    (key_grad, value_grad), query_grad = lax.scan(
        visit_block, (empty_grad, empty_grad), (query_blocks, grad_blocks)
    )
    return (query_grad.reshape(-1, head_width), key_grad, value_grad)


def owner_rows(key_parts, value_parts, token_parts, groups, row_count):
    got_key, got_value = (
        lax.all_to_all(key_parts, "seq", split_axis=0, concat_axis=0, tiled=True),
        lax.all_to_all(value_parts, "seq", split_axis=0, concat_axis=0, tiled=True),
    )

    def fold_parts(values):
        shaped = values.reshape(token_parts, groups, row_count, values.shape[2], values.shape[3])
        summed = jnp.sum(shaped, axis=0)
        return summed.transpose(1, 0, 2, 3).reshape(row_count, -1)

    return (fold_parts(got_key), fold_parts(got_value))


def pool_matrix(slots, weights, local_tokens):
    positions = jnp.arange(local_tokens)
    onehot = (slots[:, :, None] == positions[None, None, :]).astype(jnp.float32)
    return jnp.einsum("cjt,cj->tc", onehot, weights, precision=lax.Precision.HIGHEST)


def apply_pool(matrix, key_rows, value_rows):
    stacked = jnp.concatenate([key_rows, value_rows], axis=1)
    return jnp.dot(
        matrix, stacked, precision=lax.Precision.HIGHEST, preferred_element_type=jnp.float32
    )


def per_device(query, dout, mem_key, mem_value, keep_count, keep_slot, pool_weight):
    devices = lax.axis_size("seq")
    head_width = HEAD_DIM
    head_count = query.shape[2] // head_width
    groups = math.gcd(head_count, devices)
    token_parts = devices // groups
    group_heads = head_count // groups
    local_tokens = query.shape[1]
    part_rows = local_tokens // token_parts
    capacity = mem_key.shape[1]
    owner_counts = keep_count[0]

    def token_layout(values):
        shaped = values.reshape(token_parts, part_rows, groups, group_heads, head_width)
        return shaped.transpose(0, 2, 1, 3, 4).reshape(devices, part_rows, group_heads, head_width)

    def memory_layout(values):
        row_count = values.shape[0]
        shaped = values.reshape(row_count, groups, group_heads, head_width).transpose(1, 0, 2, 3)
        spread = jnp.broadcast_to(shaped[None], (token_parts,) + shaped.shape)
        return spread.reshape(devices, row_count, group_heads, head_width)

    slot_index = jnp.arange(devices * capacity)
    live_mask = slot_index % capacity < jnp.repeat(owner_counts, capacity)
    key_used, value_used = (mem_key[0], mem_value[0])
    query_rows = lax.all_to_all(
        token_layout(query[0]), "seq", split_axis=0, concat_axis=0, tiled=True
    )
    grad_rows = lax.all_to_all(
        token_layout(dout[0]), "seq", split_axis=0, concat_axis=0, tiled=True
    )
    key_rows = lax.all_to_all(
        memory_layout(key_used), "seq", split_axis=0, concat_axis=0, tiled=True
    )
    value_rows = lax.all_to_all(
        memory_layout(value_used), "seq", split_axis=0, concat_axis=0, tiled=True
    )
    item_heads = query_rows.shape[2]
    row_count = key_rows.shape[1]
    query_total = devices * part_rows
    block_rows = 512
    query_flat = jnp.moveaxis(query_rows.reshape(query_total, item_heads, head_width), 1, 0)
    grad_flat = jnp.moveaxis(grad_rows.reshape(query_total, item_heads, head_width), 1, 0)
    key_flat = jnp.moveaxis(key_rows.reshape(devices * row_count, item_heads, head_width), 1, 0)
    value_flat = jnp.moveaxis(value_rows.reshape(devices * row_count, item_heads, head_width), 1, 0)

    def one_head(pieces):
        return head_backward(pieces[0], pieces[1], pieces[2], pieces[3], live_mask, block_rows)

    query_grad, key_grad, value_grad = lax.map(
        one_head, (query_flat, grad_flat, key_flat, value_flat)
    )
    query_back = jnp.moveaxis(query_grad, 0, 1).reshape(devices, part_rows, item_heads, head_width)
    key_back = jnp.moveaxis(key_grad, 0, 1).reshape(devices, row_count, item_heads, head_width)
    value_back = jnp.moveaxis(value_grad, 0, 1).reshape(devices, row_count, item_heads, head_width)
    returned = lax.all_to_all(query_back, "seq", split_axis=0, concat_axis=0, tiled=True)
    returned = returned.reshape(token_parts, groups, part_rows, group_heads, head_width).transpose(
        0, 2, 1, 3, 4
    )
    dquery = returned.reshape(1, local_tokens, groups * group_heads * head_width)
    matrix = pool_matrix(keep_slot[0], pool_weight[0], local_tokens)
    key_rows, value_rows = owner_rows(key_back, value_back, token_parts, groups, capacity)
    local_grad = apply_pool(matrix, key_rows, value_rows).astype(jnp.bfloat16)
    tokens_grad = passed_along(local_grad, "span", -1)
    feature_width = groups * group_heads * head_width
    dkey_tok = tokens_grad[None, :, :feature_width]
    dvalue_tok = tokens_grad[None, :, feature_width:]
    return (dquery, dkey_tok, dvalue_tok)


def copy_to(src, dst, send_sem, recv_sem, seq, span):
    return pltpu.make_async_remote_copy(
        src_ref=src,
        dst_ref=dst,
        send_sem=send_sem,
        recv_sem=recv_sem,
        device_id={"seq": seq, "span": span},
        device_id_type=pl.DeviceIdType.MESH,
    )


def fused_kernel(
    q_hbm, g_hbm, k_hbm, v_hbm, count_ref, slot_ref, weight_ref,
    dq_ref, dk_ref, dv_ref,
    k_ref, v_ref, kvin, rows, kv, q_all, g_all, picks_ref, dq_out,
    acc, pair_send, pair_got, cross_send, cross_got, back_send, back, pool_send, pool_got,
    in_sem, a_send, a_recv, z_send, z_recv, q_send, q_recv, g_send, g_recv, d_send, d_recv,
    pair_sems, cross_sems, b_send, b_recv, p_send, p_recv,
):
    n = 16
    lines = 4
    parts = kv.shape[0]
    wide = HEAD_DIM
    two = 2 * wide
    quarter = q_all.shape[2]
    me = lax.axis_index("seq")
    span = lax.axis_index("span")
    other = 1 - span
    capacity = k_ref.shape[0]
    z, y, x = me // 4, (me // 2) % 2, me % 2
    own_line = me % 4
    x_line = own_line + 1 - 2 * x
    y_line = own_line + 2 - 4 * y
    d_line = 3 - own_line
    plane = (x_line, y_line, d_line)
    parity = z % 2
    half = z // 2
    in_half = me % 8
    middle = (z == 1) | (z == 2)
    z_pair = z + 1 - 2 * parity
    z_middle = 2 - half
    z_far = 3 - 3 * half
    z_near = 2 - half
    z_cross = (z + 2) % 4
    scale = HEAD_DIM ** (-0.5)
    to_exp2 = scale * math.log2(math.e)
    last = (((1,), (1,)), ((), ()))
    first = (((0,), (0,)), ((), ()))

    loads = [
        pltpu.make_async_copy(k_hbm, k_ref, in_sem.at[0]),
        pltpu.make_async_copy(v_hbm, v_ref, in_sem.at[1]),
    ]
    own_quarter = pl.ds(pl.multiple_of(own_line * quarter, 128), quarter)
    own_loads = [
        pltpu.make_async_copy(q_hbm.at[:, own_quarter], q_all.at[own_line], in_sem.at[2]),
        pltpu.make_async_copy(g_hbm.at[:, own_quarter], g_all.at[own_line], in_sem.at[3]),
    ]
    for load in loads + own_loads:
        load.start()
    barrier = pltpu.get_barrier_semaphore()
    for off in range(1, n):
        pl.semaphore_signal(
            barrier, inc=1, device_id={"seq": (me + off) % n, "span": span},
            device_id_type=pl.DeviceIdType.MESH,
        )
    for off in range(n // 2):
        pl.semaphore_signal(
            barrier, inc=1, device_id={"seq": half * 8 + (in_half + off) % 8, "span": other},
            device_id_type=pl.DeviceIdType.MESH,
        )
    for load in loads:
        load.wait()
    for p in range(n):
        source = k_ref if p < n // 2 else v_ref
        for part in range(parts):
            start = ((p % lines) * 2 * parts + 2 * part + (p // lines) % 2) * wide
            kvin[p, :, part * wide : (part + 1) * wide] = source[:, start : start + wide]
    pl.semaphore_wait(barrier, n - 1 + n // 2)

    def spread(off):
        p = (me + off) % n
        return copy_to(kvin.at[p], rows.at[me], a_send.at[off], a_recv.at[me], p, span)

    def spread_in(off):
        p = (me + off) % n
        return copy_to(kvin.at[p], rows.at[p], a_send.at[off], a_recv.at[p], p, span)

    offsets = (8, 7, 9, 6, 10, 5, 11, 4, 12, 3, 13, 2, 14, 1, 15)
    for off in offsets:
        spread(off).start()
    rows[me] = kvin[me]

    def exchange(part, t, whole, held, send_sem, recv_sem):
        line = plane[t]
        src = pl.ds(pl.multiple_of(line * quarter + part * two, 128), two)
        dst = pl.ds(part * two, two)
        return copy_to(
            whole.at[:, src], held.at[own_line, :, dst], send_sem.at[part, t], recv_sem.at[part, own_line],
            z * 4 + line, span,
        )

    def exchange_in(part, t, whole, held, send_sem, recv_sem):
        line = plane[t]
        dst = pl.ds(part * two, two)
        return copy_to(
            whole.at[:, dst], held.at[line, :, dst], send_sem.at[part, t], recv_sem.at[part, line],
            z * 4 + line, span,
        )

    queries = (q_hbm, q_all, q_send, q_recv)
    grads = (g_hbm, g_all, g_send, g_recv)
    for part in range(parts):
        for t in range(3):
            exchange(part, t, *queries).start()
            exchange(part, t, *grads).start()

    def pool_move():
        return copy_to(pool_send, pool_got, p_send, p_recv, me, other)

    @pl.when(span == 1)
    def _():
        spots = lax.broadcasted_iota(jnp.int32, pool_send.shape, 0)
        total = jnp.zeros(pool_send.shape, F32)
        for j in range(slot_ref.shape[0]):
            total = total + jnp.where(spots == slot_ref[j : j + 1, :], weight_ref[j : j + 1, :], 0.0)
        pool_send[...] = total
        pool_move().start()

    slots = n * capacity
    counts = jnp.broadcast_to(count_ref[...], (8, n)).astype(F32).astype(BF)
    owner = lax.broadcasted_iota(jnp.int32, (n, slots), 1)
    below = lax.broadcasted_iota(jnp.int32, (n, slots), 0) * capacity
    ahead = jnp.where(owner >= below + capacity, 1.0, 0.0).astype(BF)
    inside = jnp.where((owner >= below) & (owner < below + capacity), 1.0, 0.0).astype(BF)
    position = jnp.where((owner >= below) & (owner < below + capacity), owner - below, 0)
    position = jnp.sum(position.astype(F32), axis=0, keepdims=True)
    offset = jnp.dot(counts, ahead, preferred_element_type=F32)[:1]
    length = jnp.dot(counts, inside, preferred_element_type=F32)[:1]
    place = jnp.where(position < length, offset + position, -1.0).astype(jnp.int32)
    picks = lax.broadcasted_iota(jnp.int32, (LIVE, slots), 0) == place
    picks_ref[...] = jnp.where(picks, 1.0, 0.0).astype(BF)

    def along(part, source, target, k):
        block = kv.at[part, source]
        return copy_to(block, block, z_send.at[part, k], z_recv.at[part, source], target * 4 + own_line, span)

    for off in offsets:
        spread_in(off).wait_recv()
    packed = jnp.dot(picks_ref[...], rows[...].reshape(slots, parts * wide), preferred_element_type=F32)
    for part in range(parts):
        kv[part, z] = packed[:, part * wide : (part + 1) * wide].astype(BF)
        along(part, z, z_middle, 0).start()
        along(part, z, z_pair, 1).start()

    def relay(part):
        @pl.when(middle)
        def _():
            along(part, z_near, z_pair, 2).wait_recv()
            along(part, z_near, z_pair, 2).start()
            along(part, z_far, z_pair, 3).wait_recv()
            along(part, z_far, z_pair, 3).start()

    def gathered(part):
        along(part, z_pair, z_pair, 1).wait_recv()

        @pl.when(jnp.logical_not(middle))
        def _():
            along(part, z_near, z_pair, 2).wait_recv()
            along(part, z_far, z_pair, 3).wait_recv()

        for t in range(3):
            exchange_in(part, t, *queries).wait_recv()
            exchange_in(part, t, *grads).wait_recv()

    def dq_move(part, t):
        line = plane[t]
        src = pl.ds(part * two, two)
        dst = pl.ds(pl.multiple_of(own_line * quarter + part * two, 128), two)
        return copy_to(
            dq_out.at[line, :, src], dq_ref.at[:, dst], d_send.at[part, t], d_recv.at[part, own_line],
            z * 4 + line, span,
        )

    def dq_in(part, t):
        line = plane[t]
        src = pl.ds(part * two, two)
        dst = pl.ds(pl.multiple_of(line * quarter + part * two, 128), two)
        return copy_to(
            dq_out.at[line, :, src], dq_ref.at[:, dst], d_send.at[part, t], d_recv.at[part, line],
            z * 4 + line, span,
        )

    def one_head(part, b, with_memory):
        tokens = dq_out.shape[0] * dq_out.shape[1]
        here = slice((2 * part + b) * wide, (2 * part + b + 1) * wide)
        query = q_all[:, :, here].reshape(tokens, wide)
        grad = g_all[:, :, here].reshape(tokens, wide)
        key = kv[part, b]
        value = kv[part, 2 + b]
        scores = lax.dot_general(key, query, last, preferred_element_type=F32)
        shifted = jnp.exp2((scores - jnp.max(scores, axis=0, keepdims=True)) * to_exp2)
        probs = shifted * (1.0 / jnp.sum(shifted, axis=0, keepdims=True))
        low = probs.astype(BF)
        probs_grad = lax.dot_general(value, grad, last, preferred_element_type=F32)
        delta = jnp.sum(low.astype(F32) * probs_grad, axis=0, keepdims=True)
        scores_grad = (probs * (probs_grad - delta)).astype(BF)
        dq = lax.dot_general(scores_grad, key, first, preferred_element_type=F32) * scale
        dq_out[:, :, here] = dq.astype(BF).reshape(lines, tokens // lines, wide)
        if with_memory:
            acc[part, b, :, :wide] = jnp.dot(scores_grad, query, preferred_element_type=F32) * scale
            acc[part, b, :, wide:] = jnp.dot(low, grad, preferred_element_type=F32)

    def pair_move(part):
        return copy_to(
            pair_send.at[part], pair_got.at[part], pair_sems.at[part, 0], pair_sems.at[part, 1],
            z_pair * 4 + own_line, span,
        )

    def compute(part):
        @pl.when(span == 1)
        def _():
            for b in range(2):
                one_head(part, b, True)
            pair_send[part] = acc[part, 1 - parity].astype(BF)
            pair_move(part).start()

        @pl.when(span == 0)
        def _():
            for b in range(2):
                one_head(part, b, False)

        for t in range(3):
            dq_move(part, t).start()
        here = pl.ds(part * two, two)
        dst = pl.ds(pl.multiple_of(own_line * quarter + part * two, 128), two)
        dq_ref[:, dst] = dq_out[own_line, :, here]

    def cross_move(part):
        return copy_to(
            cross_send.at[part], cross_got.at[part], cross_sems.at[part, 0], cross_sems.at[part, 1],
            z_cross * 4 + own_line, span,
        )

    def cross(part):
        @pl.when(span == 1)
        def _():
            pair_move(part).wait_recv()
            total = acc[part, parity] + pair_got[part].astype(F32)
            acc[part, parity] = total
            cross_send[part] = total.astype(BF)
            cross_move(part).start()

    def give(part, off):
        p = (in_half + off) % 8
        return copy_to(
            back_send.at[part, p], back.at[part, in_half], b_send.at[part, off], b_recv.at[part, in_half],
            half * 8 + p, other,
        )

    def hand_back(part):
        @pl.when(span == 1)
        def _():
            cross_move(part).wait_recv()
            total = acc[part, parity] + cross_got[part].astype(F32)
            high = total.astype(BF)
            rest = (total - high.astype(F32)).astype(BF)
            mine = picks_ref[:, pl.ds(pl.multiple_of(half * (slots // 2), 128), slots // 2)]
            for i, value in enumerate((high, rest)):
                owned = lax.dot_general(mine, value, first, preferred_element_type=F32)
                back_send[part, :, i] = owned.astype(BF).reshape(n // 2, capacity, two)
            for off in range(n // 2):
                give(part, off).start()

    relay(0)
    relay(1)
    for load in own_loads:
        load.wait()
    gathered(0)
    compute(0)
    relay(2)
    gathered(1)
    compute(1)
    cross(0)
    gathered(2)
    compute(2)
    cross(1)
    hand_back(0)
    cross(2)
    hand_back(1)
    hand_back(2)

    @pl.when(span == 1)
    def _():
        dk_ref[...] = jnp.zeros(dk_ref.shape, BF)
        dv_ref[...] = jnp.zeros(dv_ref.shape, BF)

    @pl.when(span == 0)
    def _():
        pool_move().wait_recv()
        matrix = pool_got[...]
        high = matrix.astype(BF)
        rest = (matrix - high.astype(F32)).astype(BF)
        for part in range(parts):
            for p in range(n // 2):
                copy_to(
                    back_send.at[part, p], back.at[part, p], b_send.at[part, p], b_recv.at[part, p], me, other
                ).wait_recv()
                upper = back[part, p, 0]
                lower = back[part, p, 1]
                tokens = jnp.dot(high, lower, preferred_element_type=F32)
                tokens = tokens + jnp.dot(rest, upper, preferred_element_type=F32)
                tokens = (tokens + jnp.dot(high, upper, preferred_element_type=F32)).astype(BF)
                start = ((p % lines) * 2 * parts + 2 * part + p // lines) * wide
                dk_ref[:, start : start + wide] = tokens[:, :wide]
                dv_ref[:, start : start + wide] = tokens[:, wide:]

    for part in range(parts):
        for t in range(3):
            dq_in(part, t).wait_recv()
    for off in offsets:
        spread(off).wait_send()
    for part in range(parts):
        for t in range(3):
            exchange(part, t, *queries).wait_send()
            exchange(part, t, *grads).wait_send()
            dq_move(part, t).wait_send()
        along(part, z, z_middle, 0).wait_send()
        along(part, z, z_pair, 1).wait_send()

    @pl.when(middle)
    def _():
        for part in range(parts):
            along(part, z_near, z_pair, 2).wait_send()
            along(part, z_far, z_pair, 3).wait_send()

    @pl.when(span == 1)
    def _():
        pool_move().wait_send()
        for part in range(parts):
            pair_move(part).wait_send()
            cross_move(part).wait_send()
            for off in range(n // 2):
                give(part, off).wait_send()


def per_device_fused(query, dout, mem_key, mem_value, keep_count, keep_slot, pool_weight):
    n = 16
    lines = 4
    tokens, width = query.shape[1:]
    capacity = mem_key.shape[1]
    quarter = width // lines
    parts = quarter // (2 * HEAD_DIM)
    vmem = pl.BlockSpec(memory_space=pltpu.VMEM)
    hbm = pl.BlockSpec(memory_space=pl.ANY)
    dma = pltpu.SemaphoreType.DMA
    out = jax.ShapeDtypeStruct((tokens, width), BF)
    two = 2 * HEAD_DIM
    owned = (parts, n // 2, 2, capacity, two)
    dq, dk, dv = pl.pallas_call(
        fused_kernel,
        out_shape=(out, out, out),
        in_specs=[hbm] * 4 + [vmem] * 3,
        out_specs=(vmem, vmem, vmem),
        scratch_shapes=[
            pltpu.VMEM((capacity, width), BF),
            pltpu.VMEM((capacity, width), BF),
            pltpu.VMEM((n, capacity, parts * HEAD_DIM), BF),
            pltpu.VMEM((n, capacity, parts * HEAD_DIM), BF),
            pltpu.VMEM((parts, 4, LIVE, HEAD_DIM), BF),
            pltpu.VMEM((lines, tokens, quarter), BF),
            pltpu.VMEM((lines, tokens, quarter), BF),
            pltpu.VMEM((LIVE, n * capacity), BF),
            pltpu.VMEM((lines, tokens, quarter), BF),
            pltpu.VMEM((parts, 2, LIVE, two), F32),
            pltpu.VMEM((parts, LIVE, two), BF),
            pltpu.VMEM((parts, LIVE, two), BF),
            pltpu.VMEM((parts, LIVE, two), BF),
            pltpu.VMEM((parts, LIVE, two), BF),
            pltpu.VMEM(owned, BF),
            pltpu.VMEM(owned, BF),
            pltpu.VMEM((tokens, capacity), F32),
            pltpu.VMEM((tokens, capacity), F32),
            dma((4,)), dma((n,)), dma((n,)), dma((parts, 4)), dma((parts, 4)),
            dma((parts, 3)), dma((parts, lines)), dma((parts, 3)), dma((parts, lines)),
            dma((parts, 3)), dma((parts, lines)),
            dma((parts, 2)), dma((parts, 2)), dma((parts, n // 2)), dma((parts, n // 2)), dma, dma,
        ],
        compiler_params=pltpu.CompilerParams(
            collective_id=0, has_side_effects=True, vmem_limit_bytes=32 << 20
        ),
    )(
        query[0], dout[0], mem_key[0], mem_value[0], keep_count, keep_slot[0].T, pool_weight[0].T,
    )
    return dq[None], dk[None], dv[None]


def solution(mesh):
    fused = mesh.shape["seq"] == 16 and mesh.shape["span"] == 2
    return jax.shard_map(
        per_device_fused if fused else per_device,
        mesh=mesh,
        in_specs=(
            P("span", "seq", None),
            P("span", "seq", None),
            P("span", "seq", None),
            P("span", "seq", None),
            P("span", None),
            P("span", "seq", None),
            P("span", "seq", None),
        ),
        out_specs=(P("span", "seq", None), P("span", "seq", None), P("span", "seq", None)),
        check_vma=False,
    )
```

```python
import math

import jax
import jax.numpy as jnp
from jax import lax
from jax.experimental import pallas as pl
from jax.experimental.pallas import tpu as pltpu
from jax.sharding import PartitionSpec as P

HEAD_DIM = 128
LIVE = 256
BF = jnp.bfloat16
F32 = jnp.float32


def passed_along(block, axis, distance):
    devices = range(lax.axis_size(axis))
    route = [(i - distance, i) for i in devices if i - distance in devices]
    return lax.ppermute(block, axis, route)


def head_backward(query_head, grad_head, key_head, value_head, live_mask, block_rows):
    score_scale = key_head.shape[1] ** (-0.5)
    head_width = query_head.shape[1]
    blocks = query_head.shape[0] // block_rows
    query_blocks = query_head.reshape(blocks, block_rows, head_width)
    grad_blocks = grad_head.reshape(blocks, block_rows, head_width)

    def visit_block(totals, inputs):
        key_grad, value_grad = totals
        query_block, grad_block = inputs
        scores = jnp.dot(query_block, key_head.T, preferred_element_type=jnp.float32) * score_scale
        scores = jnp.where(live_mask[None, :], scores, -jnp.inf)
        shifted = jnp.exp(scores - jnp.max(scores, axis=1, keepdims=True))
        probs_full = shifted / jnp.sum(shifted, axis=1, keepdims=True)
        probs_low = probs_full.astype(jnp.bfloat16)
        attn_out = jnp.dot(probs_low, value_head, preferred_element_type=jnp.float32)
        deltas = jnp.sum(grad_block.astype(jnp.float32) * attn_out, axis=1, keepdims=True)
        probs_grad = jnp.dot(grad_block, value_head.T, preferred_element_type=jnp.float32)
        scores_grad = (probs_full * (probs_grad - deltas)).astype(jnp.bfloat16)
        query_grad = (
            jnp.dot(scores_grad, key_head, preferred_element_type=jnp.float32) * score_scale
        ).astype(jnp.bfloat16)
        key_grad = (
            key_grad
            + lax.dot_general(
                scores_grad,
                query_block,
                (((0,), (0,)), ((), ())),
                preferred_element_type=jnp.float32,
            )
            * score_scale
        )
        value_grad = value_grad + lax.dot_general(
            probs_low, grad_block, (((0,), (0,)), ((), ())), preferred_element_type=jnp.float32
        )
        return ((key_grad, value_grad), query_grad)

    empty_grad = jnp.zeros(key_head.shape, jnp.float32)
    (key_grad, value_grad), query_grad = lax.scan(
        visit_block, (empty_grad, empty_grad), (query_blocks, grad_blocks)
    )
    return (query_grad.reshape(-1, head_width), key_grad, value_grad)


def owner_rows(key_parts, value_parts, token_parts, groups, row_count):
    got_key, got_value = (
        lax.all_to_all(key_parts, "seq", split_axis=0, concat_axis=0, tiled=True),
        lax.all_to_all(value_parts, "seq", split_axis=0, concat_axis=0, tiled=True),
    )

    def fold_parts(values):
        shaped = values.reshape(token_parts, groups, row_count, values.shape[2], values.shape[3])
        summed = jnp.sum(shaped, axis=0)
        return summed.transpose(1, 0, 2, 3).reshape(row_count, -1)

    return (fold_parts(got_key), fold_parts(got_value))


def pool_matrix(slots, weights, local_tokens):
    positions = jnp.arange(local_tokens)
    onehot = (slots[:, :, None] == positions[None, None, :]).astype(jnp.float32)
    return jnp.einsum("cjt,cj->tc", onehot, weights, precision=lax.Precision.HIGHEST)


def apply_pool(matrix, key_rows, value_rows):
    stacked = jnp.concatenate([key_rows, value_rows], axis=1)
    return jnp.dot(
        matrix, stacked, precision=lax.Precision.HIGHEST, preferred_element_type=jnp.float32
    )


def per_device(query, dout, mem_key, mem_value, keep_count, keep_slot, pool_weight):
    devices = lax.axis_size("seq")
    head_width = HEAD_DIM
    head_count = query.shape[2] // head_width
    groups = math.gcd(head_count, devices)
    token_parts = devices // groups
    group_heads = head_count // groups
    local_tokens = query.shape[1]
    part_rows = local_tokens // token_parts
    capacity = mem_key.shape[1]
    owner_counts = keep_count[0]

    def token_layout(values):
        shaped = values.reshape(token_parts, part_rows, groups, group_heads, head_width)
        return shaped.transpose(0, 2, 1, 3, 4).reshape(devices, part_rows, group_heads, head_width)

    def memory_layout(values):
        row_count = values.shape[0]
        shaped = values.reshape(row_count, groups, group_heads, head_width).transpose(1, 0, 2, 3)
        spread = jnp.broadcast_to(shaped[None], (token_parts,) + shaped.shape)
        return spread.reshape(devices, row_count, group_heads, head_width)

    slot_index = jnp.arange(devices * capacity)
    live_mask = slot_index % capacity < jnp.repeat(owner_counts, capacity)
    key_used, value_used = (mem_key[0], mem_value[0])
    query_rows = lax.all_to_all(
        token_layout(query[0]), "seq", split_axis=0, concat_axis=0, tiled=True
    )
    grad_rows = lax.all_to_all(
        token_layout(dout[0]), "seq", split_axis=0, concat_axis=0, tiled=True
    )
    key_rows = lax.all_to_all(
        memory_layout(key_used), "seq", split_axis=0, concat_axis=0, tiled=True
    )
    value_rows = lax.all_to_all(
        memory_layout(value_used), "seq", split_axis=0, concat_axis=0, tiled=True
    )
    item_heads = query_rows.shape[2]
    row_count = key_rows.shape[1]
    query_total = devices * part_rows
    block_rows = 512
    query_flat = jnp.moveaxis(query_rows.reshape(query_total, item_heads, head_width), 1, 0)
    grad_flat = jnp.moveaxis(grad_rows.reshape(query_total, item_heads, head_width), 1, 0)
    key_flat = jnp.moveaxis(key_rows.reshape(devices * row_count, item_heads, head_width), 1, 0)
    value_flat = jnp.moveaxis(value_rows.reshape(devices * row_count, item_heads, head_width), 1, 0)

    def one_head(pieces):
        return head_backward(pieces[0], pieces[1], pieces[2], pieces[3], live_mask, block_rows)

    query_grad, key_grad, value_grad = lax.map(
        one_head, (query_flat, grad_flat, key_flat, value_flat)
    )
    query_back = jnp.moveaxis(query_grad, 0, 1).reshape(devices, part_rows, item_heads, head_width)
    key_back = jnp.moveaxis(key_grad, 0, 1).reshape(devices, row_count, item_heads, head_width)
    value_back = jnp.moveaxis(value_grad, 0, 1).reshape(devices, row_count, item_heads, head_width)
    returned = lax.all_to_all(query_back, "seq", split_axis=0, concat_axis=0, tiled=True)
    returned = returned.reshape(token_parts, groups, part_rows, group_heads, head_width).transpose(
        0, 2, 1, 3, 4
    )
    dquery = returned.reshape(1, local_tokens, groups * group_heads * head_width)
    matrix = pool_matrix(keep_slot[0], pool_weight[0], local_tokens)
    key_rows, value_rows = owner_rows(key_back, value_back, token_parts, groups, capacity)
    local_grad = apply_pool(matrix, key_rows, value_rows).astype(jnp.bfloat16)
    tokens_grad = passed_along(local_grad, "span", -1)
    feature_width = groups * group_heads * head_width
    dkey_tok = tokens_grad[None, :, :feature_width]
    dvalue_tok = tokens_grad[None, :, feature_width:]
    return (dquery, dkey_tok, dvalue_tok)


def copy_to(src, dst, send_sem, recv_sem, seq, span):
    return pltpu.make_async_remote_copy(
        src_ref=src,
        dst_ref=dst,
        send_sem=send_sem,
        recv_sem=recv_sem,
        device_id={"seq": seq, "span": span},
        device_id_type=pl.DeviceIdType.MESH,
    )


def fused_kernel(
    q_hbm, g_hbm, k_hbm, v_hbm, count_hbm, slot_hbm, weight_hbm,
    dq_hbm, dk_hbm, dv_hbm,
    count_ref, slot_ref, weight_ref, k_ref, v_ref, kvin, rows, kv, q_all, g_all, picks_ref, dq_out, dk_ref, dv_ref,
    acc, pair_send, pair_got, cross_send, cross_got, back_send, back, pool_send, pool_got,
    in_sem, a_send, a_recv, z_send, z_recv, q_send, q_recv, g_send, g_recv, d_send, d_recv,
    pair_sems, cross_sems, b_send, b_recv, p_send, p_recv, dq_sem, out_sem,
):
    n = 16
    lines = 4
    parts = kv.shape[0]
    wide = HEAD_DIM
    two = 2 * wide
    quarter = q_all.shape[2]
    me = lax.axis_index("seq")
    span = lax.axis_index("span")
    other = 1 - span
    capacity = k_ref.shape[0]
    z, y, x = me // 4, (me // 2) % 2, me % 2
    own_line = me % 4
    x_line = own_line + 1 - 2 * x
    y_line = own_line + 2 - 4 * y
    d_line = 3 - own_line
    plane = (x_line, y_line, d_line)
    parity = z % 2
    half = z // 2
    in_half = me % 8
    middle = (z == 1) | (z == 2)
    z_pair = z + 1 - 2 * parity
    z_middle = 2 - half
    z_far = 3 - 3 * half
    z_near = 2 - half
    z_cross = (z + 2) % 4
    scale = HEAD_DIM ** (-0.5)
    to_exp2 = scale * math.log2(math.e)
    last = (((1,), (1,)), ((), ()))
    first = (((0,), (0,)), ((), ()))

    loads = [
        pltpu.make_async_copy(k_hbm, k_ref, in_sem.at[0]),
        pltpu.make_async_copy(v_hbm, v_ref, in_sem.at[1]),
    ]
    own_quarter = pl.ds(pl.multiple_of(own_line * quarter, 128), quarter)
    own_loads = [
        pltpu.make_async_copy(q_hbm.at[:, own_quarter], q_all.at[own_line], in_sem.at[2]),
        pltpu.make_async_copy(g_hbm.at[:, own_quarter], g_all.at[own_line], in_sem.at[3]),
    ]
    small_loads = [
        pltpu.make_async_copy(count_hbm, count_ref, in_sem.at[4]),
        pltpu.make_async_copy(slot_hbm, slot_ref, in_sem.at[5]),
        pltpu.make_async_copy(weight_hbm, weight_ref, in_sem.at[6]),
    ]
    for load in loads + small_loads + own_loads:
        load.start()
    barrier = pltpu.get_barrier_semaphore()
    for off in range(1, n):
        pl.semaphore_signal(
            barrier, inc=1, device_id={"seq": (me + off) % n, "span": span},
            device_id_type=pl.DeviceIdType.MESH,
        )
    for off in range(n // 2):
        pl.semaphore_signal(
            barrier, inc=1, device_id={"seq": half * 8 + (in_half + off) % 8, "span": other},
            device_id_type=pl.DeviceIdType.MESH,
        )
    for load in loads + small_loads:
        load.wait()
    for p in range(n):
        source = k_ref if p < n // 2 else v_ref
        for part in range(parts):
            start = ((p % lines) * 2 * parts + 2 * part + (p // lines) % 2) * wide
            kvin[p, :, part * wide : (part + 1) * wide] = source[:, start : start + wide]
    pl.semaphore_wait(barrier, n - 1 + n // 2)

    def spread(off):
        p = (me + off) % n
        return copy_to(kvin.at[p], rows.at[me], a_send.at[off], a_recv.at[me], p, span)

    def spread_in(off):
        p = (me + off) % n
        return copy_to(kvin.at[p], rows.at[p], a_send.at[off], a_recv.at[p], p, span)

    offsets = (8, 7, 9, 6, 10, 5, 11, 4, 12, 3, 13, 2, 14, 1, 15)
    for off in offsets:
        spread(off).start()
    rows[me] = kvin[me]

    def exchange(part, t, whole, held, send_sem, recv_sem):
        line = plane[t]
        src = pl.ds(pl.multiple_of(line * quarter + part * two, 128), two)
        dst = pl.ds(part * two, two)
        return copy_to(
            whole.at[:, src], held.at[own_line, :, dst], send_sem.at[part, t], recv_sem.at[part, own_line],
            z * 4 + line, span,
        )

    def exchange_in(part, t, whole, held, send_sem, recv_sem):
        line = plane[t]
        dst = pl.ds(part * two, two)
        return copy_to(
            whole.at[:, dst], held.at[line, :, dst], send_sem.at[part, t], recv_sem.at[part, line],
            z * 4 + line, span,
        )

    queries = (q_hbm, q_all, q_send, q_recv)
    grads = (g_hbm, g_all, g_send, g_recv)
    for part in range(parts):
        for t in range(3):
            exchange(part, t, *queries).start()
            exchange(part, t, *grads).start()

    def pool_move():
        return copy_to(pool_send, pool_got, p_send, p_recv, me, other)

    @pl.when(span == 1)
    def _():
        spots = lax.broadcasted_iota(jnp.int32, pool_send.shape, 0)
        total = jnp.zeros(pool_send.shape, F32)
        for j in range(slot_ref.shape[0]):
            total = total + jnp.where(spots == slot_ref[j : j + 1, :], weight_ref[j : j + 1, :], 0.0)
        pool_send[...] = total
        pool_move().start()

    slots = n * capacity
    counts = jnp.broadcast_to(count_ref[...], (8, n)).astype(F32).astype(BF)
    owner = lax.broadcasted_iota(jnp.int32, (n, slots), 1)
    below = lax.broadcasted_iota(jnp.int32, (n, slots), 0) * capacity
    ahead = jnp.where(owner >= below + capacity, 1.0, 0.0).astype(BF)
    inside = jnp.where((owner >= below) & (owner < below + capacity), 1.0, 0.0).astype(BF)
    position = jnp.where((owner >= below) & (owner < below + capacity), owner - below, 0)
    position = jnp.sum(position.astype(F32), axis=0, keepdims=True)
    offset = jnp.dot(counts, ahead, preferred_element_type=F32)[:1]
    length = jnp.dot(counts, inside, preferred_element_type=F32)[:1]
    place = jnp.where(position < length, offset + position, -1.0).astype(jnp.int32)
    picks = lax.broadcasted_iota(jnp.int32, (LIVE, slots), 0) == place
    picks_ref[...] = jnp.where(picks, 1.0, 0.0).astype(BF)

    def along(part, source, target, k):
        block = kv.at[part, source]
        return copy_to(block, block, z_send.at[part, k], z_recv.at[part, source], target * 4 + own_line, span)

    for off in offsets:
        spread_in(off).wait_recv()
    packed = jnp.dot(picks_ref[...], rows[...].reshape(slots, parts * wide), preferred_element_type=F32)
    for part in range(parts):
        kv[part, z] = packed[:, part * wide : (part + 1) * wide].astype(BF)
        along(part, z, z_middle, 0).start()
        along(part, z, z_pair, 1).start()

    def relay(part):
        @pl.when(middle)
        def _():
            along(part, z_near, z_pair, 2).wait_recv()
            along(part, z_near, z_pair, 2).start()
            along(part, z_far, z_pair, 3).wait_recv()
            along(part, z_far, z_pair, 3).start()

    def gathered(part):
        along(part, z_pair, z_pair, 1).wait_recv()

        @pl.when(jnp.logical_not(middle))
        def _():
            along(part, z_near, z_pair, 2).wait_recv()
            along(part, z_far, z_pair, 3).wait_recv()

        for t in range(3):
            exchange_in(part, t, *queries).wait_recv()
            exchange_in(part, t, *grads).wait_recv()

    def dq_move(part, t):
        line = plane[t]
        src = pl.ds(part * two, two)
        dst = pl.ds(pl.multiple_of(own_line * quarter + part * two, 128), two)
        return copy_to(
            dq_out.at[line, :, src], dq_hbm.at[:, dst], d_send.at[part, t], d_recv.at[part, own_line],
            z * 4 + line, span,
        )

    def dq_in(part, t):
        line = plane[t]
        src = pl.ds(part * two, two)
        dst = pl.ds(pl.multiple_of(line * quarter + part * two, 128), two)
        return copy_to(
            dq_out.at[line, :, src], dq_hbm.at[:, dst], d_send.at[part, t], d_recv.at[part, line],
            z * 4 + line, span,
        )

    def one_head(part, b, with_memory):
        tokens = dq_out.shape[0] * dq_out.shape[1]
        here = slice((2 * part + b) * wide, (2 * part + b + 1) * wide)
        query = q_all[:, :, here].reshape(tokens, wide)
        grad = g_all[:, :, here].reshape(tokens, wide)
        key = kv[part, b]
        value = kv[part, 2 + b]
        scores = lax.dot_general(key, query, last, preferred_element_type=F32)
        shifted = jnp.exp2((scores - jnp.max(scores, axis=0, keepdims=True)) * to_exp2)
        probs = shifted * (1.0 / jnp.sum(shifted, axis=0, keepdims=True))
        low = probs.astype(BF)
        probs_grad = lax.dot_general(value, grad, last, preferred_element_type=F32)
        delta = jnp.sum(low.astype(F32) * probs_grad, axis=0, keepdims=True)
        scores_grad = (probs * (probs_grad - delta)).astype(BF)
        dq = lax.dot_general(scores_grad, key, first, preferred_element_type=F32) * scale
        dq_out[:, :, here] = dq.astype(BF).reshape(lines, tokens // lines, wide)
        if with_memory:
            acc[part, b, :, :wide] = jnp.dot(scores_grad, query, preferred_element_type=F32) * scale
            acc[part, b, :, wide:] = jnp.dot(low, grad, preferred_element_type=F32)

    def pair_move(part):
        return copy_to(
            pair_send.at[part], pair_got.at[part], pair_sems.at[part, 0], pair_sems.at[part, 1],
            z_pair * 4 + own_line, span,
        )

    def compute(part):
        @pl.when(span == 1)
        def _():
            for b in range(2):
                one_head(part, b, True)
            pair_send[part] = acc[part, 1 - parity].astype(BF)
            pair_move(part).start()

        @pl.when(span == 0)
        def _():
            for b in range(2):
                one_head(part, b, False)

        for t in range(3):
            dq_move(part, t).start()

    keep = pltpu.make_async_copy(dq_out.at[own_line], dq_hbm.at[:, own_quarter], dq_sem)

    def put(lo, hi, line, which):
        here = pl.ds((line * parts + lo) * two, (hi - lo) * two)
        src, dst = ((dk_ref, dk_hbm), (dv_ref, dv_hbm))[which]
        return pltpu.make_async_copy(src.at[:, here], dst.at[:, here], out_sem.at[which, line, lo])

    def cross_move(part):
        return copy_to(
            cross_send.at[part], cross_got.at[part], cross_sems.at[part, 0], cross_sems.at[part, 1],
            z_cross * 4 + own_line, span,
        )

    def cross(part):
        @pl.when(span == 1)
        def _():
            pair_move(part).wait_recv()
            total = acc[part, parity] + pair_got[part].astype(F32)
            acc[part, parity] = total
            cross_send[part] = total.astype(BF)
            cross_move(part).start()

    def give(part, off):
        p = (in_half + off) % 8
        return copy_to(
            back_send.at[part, p], back.at[part, in_half], b_send.at[part, off], b_recv.at[part, in_half],
            half * 8 + p, other,
        )

    def hand_back(part):
        @pl.when(span == 1)
        def _():
            cross_move(part).wait_recv()
            total = acc[part, parity] + cross_got[part].astype(F32)
            high = total.astype(BF)
            rest = (total - high.astype(F32)).astype(BF)
            mine = picks_ref[:, pl.ds(pl.multiple_of(half * (slots // 2), 128), slots // 2)]
            for i, value in enumerate((high, rest)):
                owned = lax.dot_general(mine, value, first, preferred_element_type=F32)
                back_send[part, :, i] = owned.astype(BF).reshape(n // 2, capacity, two)
            for off in range(n // 2):
                give(part, off).start()

    zeros = [
        pltpu.make_async_copy(dk_ref, dst, out_sem.at[which, 0, 0])
        for which, dst in enumerate((dk_hbm, dv_hbm))
    ]

    @pl.when(span == 1)
    def _():
        dk_ref[...] = jnp.zeros(dk_ref.shape, BF)
        for zero in zeros:
            zero.start()

    relay(0)
    relay(1)
    for load in own_loads:
        load.wait()
    gathered(0)
    compute(0)
    relay(2)
    gathered(1)
    compute(1)
    cross(0)
    gathered(2)
    compute(2)
    keep.start()
    cross(1)
    hand_back(0)
    cross(2)
    hand_back(1)
    hand_back(2)

    @pl.when(span == 0)
    def _():
        pool_move().wait_recv()
        matrix = pool_got[...]
        high = matrix.astype(BF)
        rest = (matrix - high.astype(F32)).astype(BF)
        for part in range(parts):
            for p in range(n // 2):
                copy_to(
                    back_send.at[part, p], back.at[part, p], b_send.at[part, p], b_recv.at[part, p], me, other
                ).wait_recv()
                upper = back[part, p, 0]
                lower = back[part, p, 1]
                tokens = jnp.dot(high, lower, preferred_element_type=F32)
                tokens = tokens + jnp.dot(rest, upper, preferred_element_type=F32)
                tokens = (tokens + jnp.dot(high, upper, preferred_element_type=F32)).astype(BF)
                start = ((p % lines) * 2 * parts + 2 * part + p // lines) * wide
                dk_ref[:, start : start + wide] = tokens[:, :wide]
                dv_ref[:, start : start + wide] = tokens[:, wide:]
            if part > 0:
                for line in range(lines):
                    for which in range(2):
                        put(0 if part == 1 else part, part + 1, line, which).start()

    for part in range(parts):
        for t in range(3):
            dq_in(part, t).wait_recv()
    keep.wait()

    @pl.when(span == 0)
    def _():
        for line in range(lines):
            for which in range(2):
                put(0, 2, line, which).wait()
                for part in range(2, parts):
                    put(part, part + 1, line, which).wait()

    for off in offsets:
        spread(off).wait_send()
    for part in range(parts):
        for t in range(3):
            exchange(part, t, *queries).wait_send()
            exchange(part, t, *grads).wait_send()
            dq_move(part, t).wait_send()
        along(part, z, z_middle, 0).wait_send()
        along(part, z, z_pair, 1).wait_send()

    @pl.when(middle)
    def _():
        for part in range(parts):
            along(part, z_near, z_pair, 2).wait_send()
            along(part, z_far, z_pair, 3).wait_send()

    @pl.when(span == 1)
    def _():
        pool_move().wait_send()
        for zero in zeros:
            zero.wait()
        for part in range(parts):
            pair_move(part).wait_send()
            cross_move(part).wait_send()
            for off in range(n // 2):
                give(part, off).wait_send()


def settle_kernel(dq_in, dk_in, dv_in, dq_ref, dk_ref, dv_ref, held, sems):
    pairs = ((dq_in, dq_ref), (dk_in, dk_ref), (dv_in, dv_ref))
    loads = [pltpu.make_async_copy(src, held.at[i], sems.at[0, i]) for i, (src, _) in enumerate(pairs)]
    stores = [pltpu.make_async_copy(held.at[i], dst, sems.at[1, i]) for i, (_, dst) in enumerate(pairs)]
    for load in loads:
        load.start()
    for load, store in zip(loads, stores):
        load.wait()
        store.start()
    for store in stores:
        store.wait()


def per_device_fused(query, dout, mem_key, mem_value, keep_count, keep_slot, pool_weight):
    n = 16
    lines = 4
    tokens, width = query.shape[1:]
    capacity = mem_key.shape[1]
    quarter = width // lines
    parts = quarter // (2 * HEAD_DIM)
    hbm = pl.BlockSpec(memory_space=pl.ANY)
    dma = pltpu.SemaphoreType.DMA
    out = jax.ShapeDtypeStruct((tokens, width), BF)
    two = 2 * HEAD_DIM
    owned = (parts, n // 2, 2, capacity, two)
    dq, dk, dv = pl.pallas_call(
        fused_kernel,
        out_shape=(out, out, out),
        in_specs=[hbm] * 7,
        out_specs=(hbm, hbm, hbm),
        scratch_shapes=[
            pltpu.VMEM(keep_count.shape, jnp.int32),
            pltpu.VMEM((keep_slot.shape[2], capacity), jnp.int32),
            pltpu.VMEM((keep_slot.shape[2], capacity), F32),
            pltpu.VMEM((capacity, width), BF),
            pltpu.VMEM((capacity, width), BF),
            pltpu.VMEM((n, capacity, parts * HEAD_DIM), BF),
            pltpu.VMEM((n, capacity, parts * HEAD_DIM), BF),
            pltpu.VMEM((parts, 4, LIVE, HEAD_DIM), BF),
            pltpu.VMEM((lines, tokens, quarter), BF),
            pltpu.VMEM((lines, tokens, quarter), BF),
            pltpu.VMEM((LIVE, n * capacity), BF),
            pltpu.VMEM((lines, tokens, quarter), BF),
            pltpu.VMEM((tokens, width), BF),
            pltpu.VMEM((tokens, width), BF),
            pltpu.VMEM((parts, 2, LIVE, two), F32),
            pltpu.VMEM((parts, LIVE, two), BF),
            pltpu.VMEM((parts, LIVE, two), BF),
            pltpu.VMEM((parts, LIVE, two), BF),
            pltpu.VMEM((parts, LIVE, two), BF),
            pltpu.VMEM(owned, BF),
            pltpu.VMEM(owned, BF),
            pltpu.VMEM((tokens, capacity), F32),
            pltpu.VMEM((tokens, capacity), F32),
            dma((7,)), dma((n,)), dma((n,)), dma((parts, 4)), dma((parts, 4)),
            dma((parts, 3)), dma((parts, lines)), dma((parts, 3)), dma((parts, lines)),
            dma((parts, 3)), dma((parts, lines)),
            dma((parts, 2)), dma((parts, 2)), dma((parts, n // 2)), dma((parts, n // 2)), dma, dma, dma,
            dma((2, lines, parts)),
        ],
        compiler_params=pltpu.CompilerParams(
            collective_id=0, has_side_effects=True, vmem_limit_bytes=56 << 20
        ),
    )(
        query[0], dout[0], mem_key[0], mem_value[0], keep_count, keep_slot[0].T, pool_weight[0].T,
    )
    any_space = pl.BlockSpec(memory_space=pl.ANY)
    dq, dk, dv = pl.pallas_call(
        settle_kernel,
        out_shape=(out, out, out),
        in_specs=[any_space] * 3,
        out_specs=(any_space,) * 3,
        scratch_shapes=[pltpu.VMEM((3, tokens, width), BF), dma((2, 3))],
        compiler_params=pltpu.CompilerParams(vmem_limit_bytes=56 << 20),
    )(dq, dk, dv)
    return dq[None], dk[None], dv[None]


def solution(mesh):
    fused = mesh.shape["seq"] == 16 and mesh.shape["span"] == 2
    return jax.shard_map(
        per_device_fused if fused else per_device,
        mesh=mesh,
        in_specs=(
            P("span", "seq", None),
            P("span", "seq", None),
            P("span", "seq", None),
            P("span", "seq", None),
            P("span", None),
            P("span", "seq", None),
            P("span", "seq", None),
        ),
        out_specs=(P("span", "seq", None), P("span", "seq", None), P("span", "seq", None)),
        check_vma=False,
    )
```

```python
import math

import jax
import jax.numpy as jnp
from jax import lax
from jax.experimental import pallas as pl
from jax.experimental.pallas import tpu as pltpu
from jax.sharding import PartitionSpec as P

HEAD_DIM = 128
LIVE = 256
BF = jnp.bfloat16
F32 = jnp.float32


def passed_along(block, axis, distance):
    devices = range(lax.axis_size(axis))
    route = [(i - distance, i) for i in devices if i - distance in devices]
    return lax.ppermute(block, axis, route)


def head_backward(query_head, grad_head, key_head, value_head, live_mask, block_rows):
    score_scale = key_head.shape[1] ** (-0.5)
    head_width = query_head.shape[1]
    blocks = query_head.shape[0] // block_rows
    query_blocks = query_head.reshape(blocks, block_rows, head_width)
    grad_blocks = grad_head.reshape(blocks, block_rows, head_width)

    def visit_block(totals, inputs):
        key_grad, value_grad = totals
        query_block, grad_block = inputs
        scores = jnp.dot(query_block, key_head.T, preferred_element_type=jnp.float32) * score_scale
        scores = jnp.where(live_mask[None, :], scores, -jnp.inf)
        shifted = jnp.exp(scores - jnp.max(scores, axis=1, keepdims=True))
        probs_full = shifted / jnp.sum(shifted, axis=1, keepdims=True)
        probs_low = probs_full.astype(jnp.bfloat16)
        attn_out = jnp.dot(probs_low, value_head, preferred_element_type=jnp.float32)
        deltas = jnp.sum(grad_block.astype(jnp.float32) * attn_out, axis=1, keepdims=True)
        probs_grad = jnp.dot(grad_block, value_head.T, preferred_element_type=jnp.float32)
        scores_grad = (probs_full * (probs_grad - deltas)).astype(jnp.bfloat16)
        query_grad = (
            jnp.dot(scores_grad, key_head, preferred_element_type=jnp.float32) * score_scale
        ).astype(jnp.bfloat16)
        key_grad = (
            key_grad
            + lax.dot_general(
                scores_grad,
                query_block,
                (((0,), (0,)), ((), ())),
                preferred_element_type=jnp.float32,
            )
            * score_scale
        )
        value_grad = value_grad + lax.dot_general(
            probs_low, grad_block, (((0,), (0,)), ((), ())), preferred_element_type=jnp.float32
        )
        return ((key_grad, value_grad), query_grad)

    empty_grad = jnp.zeros(key_head.shape, jnp.float32)
    (key_grad, value_grad), query_grad = lax.scan(
        visit_block, (empty_grad, empty_grad), (query_blocks, grad_blocks)
    )
    return (query_grad.reshape(-1, head_width), key_grad, value_grad)


def owner_rows(key_parts, value_parts, token_parts, groups, row_count):
    got_key, got_value = (
        lax.all_to_all(key_parts, "seq", split_axis=0, concat_axis=0, tiled=True),
        lax.all_to_all(value_parts, "seq", split_axis=0, concat_axis=0, tiled=True),
    )

    def fold_parts(values):
        shaped = values.reshape(token_parts, groups, row_count, values.shape[2], values.shape[3])
        summed = jnp.sum(shaped, axis=0)
        return summed.transpose(1, 0, 2, 3).reshape(row_count, -1)

    return (fold_parts(got_key), fold_parts(got_value))


def pool_matrix(slots, weights, local_tokens):
    positions = jnp.arange(local_tokens)
    onehot = (slots[:, :, None] == positions[None, None, :]).astype(jnp.float32)
    return jnp.einsum("cjt,cj->tc", onehot, weights, precision=lax.Precision.HIGHEST)


def apply_pool(matrix, key_rows, value_rows):
    stacked = jnp.concatenate([key_rows, value_rows], axis=1)
    return jnp.dot(
        matrix, stacked, precision=lax.Precision.HIGHEST, preferred_element_type=jnp.float32
    )


def per_device(query, dout, mem_key, mem_value, keep_count, keep_slot, pool_weight):
    devices = lax.axis_size("seq")
    head_width = HEAD_DIM
    head_count = query.shape[2] // head_width
    groups = math.gcd(head_count, devices)
    token_parts = devices // groups
    group_heads = head_count // groups
    local_tokens = query.shape[1]
    part_rows = local_tokens // token_parts
    capacity = mem_key.shape[1]
    owner_counts = keep_count[0]

    def token_layout(values):
        shaped = values.reshape(token_parts, part_rows, groups, group_heads, head_width)
        return shaped.transpose(0, 2, 1, 3, 4).reshape(devices, part_rows, group_heads, head_width)

    def memory_layout(values):
        row_count = values.shape[0]
        shaped = values.reshape(row_count, groups, group_heads, head_width).transpose(1, 0, 2, 3)
        spread = jnp.broadcast_to(shaped[None], (token_parts,) + shaped.shape)
        return spread.reshape(devices, row_count, group_heads, head_width)

    slot_index = jnp.arange(devices * capacity)
    live_mask = slot_index % capacity < jnp.repeat(owner_counts, capacity)
    key_used, value_used = (mem_key[0], mem_value[0])
    query_rows = lax.all_to_all(
        token_layout(query[0]), "seq", split_axis=0, concat_axis=0, tiled=True
    )
    grad_rows = lax.all_to_all(
        token_layout(dout[0]), "seq", split_axis=0, concat_axis=0, tiled=True
    )
    key_rows = lax.all_to_all(
        memory_layout(key_used), "seq", split_axis=0, concat_axis=0, tiled=True
    )
    value_rows = lax.all_to_all(
        memory_layout(value_used), "seq", split_axis=0, concat_axis=0, tiled=True
    )
    item_heads = query_rows.shape[2]
    row_count = key_rows.shape[1]
    query_total = devices * part_rows
    block_rows = 512
    query_flat = jnp.moveaxis(query_rows.reshape(query_total, item_heads, head_width), 1, 0)
    grad_flat = jnp.moveaxis(grad_rows.reshape(query_total, item_heads, head_width), 1, 0)
    key_flat = jnp.moveaxis(key_rows.reshape(devices * row_count, item_heads, head_width), 1, 0)
    value_flat = jnp.moveaxis(value_rows.reshape(devices * row_count, item_heads, head_width), 1, 0)

    def one_head(pieces):
        return head_backward(pieces[0], pieces[1], pieces[2], pieces[3], live_mask, block_rows)

    query_grad, key_grad, value_grad = lax.map(
        one_head, (query_flat, grad_flat, key_flat, value_flat)
    )
    query_back = jnp.moveaxis(query_grad, 0, 1).reshape(devices, part_rows, item_heads, head_width)
    key_back = jnp.moveaxis(key_grad, 0, 1).reshape(devices, row_count, item_heads, head_width)
    value_back = jnp.moveaxis(value_grad, 0, 1).reshape(devices, row_count, item_heads, head_width)
    returned = lax.all_to_all(query_back, "seq", split_axis=0, concat_axis=0, tiled=True)
    returned = returned.reshape(token_parts, groups, part_rows, group_heads, head_width).transpose(
        0, 2, 1, 3, 4
    )
    dquery = returned.reshape(1, local_tokens, groups * group_heads * head_width)
    matrix = pool_matrix(keep_slot[0], pool_weight[0], local_tokens)
    key_rows, value_rows = owner_rows(key_back, value_back, token_parts, groups, capacity)
    local_grad = apply_pool(matrix, key_rows, value_rows).astype(jnp.bfloat16)
    tokens_grad = passed_along(local_grad, "span", -1)
    feature_width = groups * group_heads * head_width
    dkey_tok = tokens_grad[None, :, :feature_width]
    dvalue_tok = tokens_grad[None, :, feature_width:]
    return (dquery, dkey_tok, dvalue_tok)


def copy_to(src, dst, send_sem, recv_sem, seq, span):
    return pltpu.make_async_remote_copy(
        src_ref=src,
        dst_ref=dst,
        send_sem=send_sem,
        recv_sem=recv_sem,
        device_id={"seq": seq, "span": span},
        device_id_type=pl.DeviceIdType.MESH,
    )


def fused_kernel(
    q_hbm, g_hbm, k_hbm, v_hbm, count_hbm, slot_hbm, weight_hbm,
    dq_ref, dk_ref, dv_ref,
    count_ref, slot_ref, weight_ref, k_ref, v_ref, kvin, rows, kv, q_all, g_all, picks_ref, dq_out,
    acc, pair_send, pair_got, cross_send, cross_got, back_send, back, pool_send, pool_got,
    in_sem, a_send, a_recv, z_send, z_recv, q_send, q_recv, g_send, g_recv, d_send, d_recv,
    pair_sems, cross_sems, b_send, b_recv, p_send, p_recv,
):
    n = 16
    lines = 4
    parts = kv.shape[0]
    wide = HEAD_DIM
    two = 2 * wide
    quarter = q_all.shape[2]
    me = lax.axis_index("seq")
    span = lax.axis_index("span")
    other = 1 - span
    capacity = k_ref.shape[0]
    z, y, x = me // 4, (me // 2) % 2, me % 2
    own_line = me % 4
    x_line = own_line + 1 - 2 * x
    y_line = own_line + 2 - 4 * y
    d_line = 3 - own_line
    plane = (x_line, y_line, d_line)
    parity = z % 2
    half = z // 2
    in_half = me % 8
    middle = (z == 1) | (z == 2)
    z_pair = z + 1 - 2 * parity
    z_middle = 2 - half
    z_far = 3 - 3 * half
    z_near = 2 - half
    z_cross = (z + 2) % 4
    scale = HEAD_DIM ** (-0.5)
    to_exp2 = scale * math.log2(math.e)
    last = (((1,), (1,)), ((), ()))
    first = (((0,), (0,)), ((), ()))

    loads = [
        pltpu.make_async_copy(k_hbm, k_ref, in_sem.at[0]),
        pltpu.make_async_copy(v_hbm, v_ref, in_sem.at[1]),
    ]
    own_quarter = pl.ds(pl.multiple_of(own_line * quarter, 128), quarter)
    own_loads = [
        pltpu.make_async_copy(q_hbm.at[:, own_quarter], q_all.at[own_line], in_sem.at[2]),
        pltpu.make_async_copy(g_hbm.at[:, own_quarter], g_all.at[own_line], in_sem.at[3]),
    ]
    small_loads = [
        pltpu.make_async_copy(count_hbm, count_ref, in_sem.at[4]),
        pltpu.make_async_copy(slot_hbm, slot_ref, in_sem.at[5]),
        pltpu.make_async_copy(weight_hbm, weight_ref, in_sem.at[6]),
    ]
    for load in loads + small_loads + own_loads:
        load.start()
    barrier = pltpu.get_barrier_semaphore()
    for off in range(1, n):
        pl.semaphore_signal(
            barrier, inc=1, device_id={"seq": (me + off) % n, "span": span},
            device_id_type=pl.DeviceIdType.MESH,
        )
    for off in range(n // 2):
        pl.semaphore_signal(
            barrier, inc=1, device_id={"seq": half * 8 + (in_half + off) % 8, "span": other},
            device_id_type=pl.DeviceIdType.MESH,
        )
    for load in loads + small_loads:
        load.wait()
    for p in range(n):
        source = k_ref if p < n // 2 else v_ref
        for part in range(parts):
            start = ((p % lines) * 2 * parts + 2 * part + (p // lines) % 2) * wide
            kvin[part, p] = source[:, start : start + wide]
    pl.semaphore_wait(barrier, n - 1 + n // 2)

    def spread(part, off):
        p = (me + off) % n
        return copy_to(kvin.at[part, p], rows.at[part, me], a_send.at[part, off], a_recv.at[part, me], p, span)

    def spread_in(part, off):
        p = (me + off) % n
        return copy_to(kvin.at[part, p], rows.at[part, p], a_send.at[part, off], a_recv.at[part, p], p, span)

    offsets = (8, 7, 9, 6, 10, 5, 11, 4, 12, 3, 13, 2, 14, 1, 15)

    def send_memory(part):
        for off in offsets:
            spread(part, off).start()
        rows[part, me] = kvin[part, me]

    def exchange(part, t, whole, held, send_sem, recv_sem):
        line = plane[t]
        src = pl.ds(pl.multiple_of(line * quarter + part * two, 128), two)
        dst = pl.ds(part * two, two)
        return copy_to(
            whole.at[:, src], held.at[own_line, :, dst], send_sem.at[part, t], recv_sem.at[part, own_line],
            z * 4 + line, span,
        )

    def exchange_in(part, t, whole, held, send_sem, recv_sem):
        line = plane[t]
        dst = pl.ds(part * two, two)
        return copy_to(
            whole.at[:, dst], held.at[line, :, dst], send_sem.at[part, t], recv_sem.at[part, line],
            z * 4 + line, span,
        )

    queries = (q_hbm, q_all, q_send, q_recv)
    grads = (g_hbm, g_all, g_send, g_recv)
    def send_tokens(part):
        for t in range(3):
            exchange(part, t, *queries).start()
            exchange(part, t, *grads).start()

    send_memory(0)
    send_tokens(0)
    send_memory(1)

    def pool_move():
        return copy_to(pool_send, pool_got, p_send, p_recv, me, other)

    @pl.when(span == 1)
    def _():
        spots = lax.broadcasted_iota(jnp.int32, pool_send.shape, 0)
        total = jnp.zeros(pool_send.shape, F32)
        for j in range(slot_ref.shape[0]):
            total = total + jnp.where(spots == slot_ref[j : j + 1, :], weight_ref[j : j + 1, :], 0.0)
        pool_send[...] = total
        pool_move().start()

    slots = n * capacity
    counts = jnp.broadcast_to(count_ref[...], (8, n)).astype(F32).astype(BF)
    owner = lax.broadcasted_iota(jnp.int32, (n, slots), 1)
    below = lax.broadcasted_iota(jnp.int32, (n, slots), 0) * capacity
    ahead = jnp.where(owner >= below + capacity, 1.0, 0.0).astype(BF)
    inside = jnp.where((owner >= below) & (owner < below + capacity), 1.0, 0.0).astype(BF)
    position = jnp.where((owner >= below) & (owner < below + capacity), owner - below, 0)
    position = jnp.sum(position.astype(F32), axis=0, keepdims=True)
    offset = jnp.dot(counts, ahead, preferred_element_type=F32)[:1]
    length = jnp.dot(counts, inside, preferred_element_type=F32)[:1]
    place = jnp.where(position < length, offset + position, -1.0).astype(jnp.int32)
    picks = lax.broadcasted_iota(jnp.int32, (LIVE, slots), 0) == place
    picks_ref[...] = jnp.where(picks, 1.0, 0.0).astype(BF)

    def along(part, source, target, k):
        block = kv.at[part, source]
        return copy_to(block, block, z_send.at[part, k], z_recv.at[part, source], target * 4 + own_line, span)

    def pack(part):
        for off in offsets:
            spread_in(part, off).wait_recv()
        packed = jnp.dot(picks_ref[...], rows[part].reshape(slots, wide), preferred_element_type=F32)
        kv[part, z] = packed.astype(BF)
        along(part, z, z_middle, 0).start()
        along(part, z, z_pair, 1).start()

    def relay(part):
        @pl.when(middle)
        def _():
            along(part, z_near, z_pair, 2).wait_recv()
            along(part, z_near, z_pair, 2).start()
            along(part, z_far, z_pair, 3).wait_recv()
            along(part, z_far, z_pair, 3).start()

    def gathered(part):
        along(part, z_pair, z_pair, 1).wait_recv()

        @pl.when(jnp.logical_not(middle))
        def _():
            along(part, z_near, z_pair, 2).wait_recv()
            along(part, z_far, z_pair, 3).wait_recv()

        for t in range(3):
            exchange_in(part, t, *queries).wait_recv()
            exchange_in(part, t, *grads).wait_recv()

    def dq_move(part, t):
        line = plane[t]
        src = pl.ds(part * two, two)
        dst = pl.ds(pl.multiple_of(own_line * quarter + part * two, 128), two)
        return copy_to(
            dq_out.at[line, :, src], dq_ref.at[:, dst], d_send.at[part, t], d_recv.at[part, own_line],
            z * 4 + line, span,
        )

    def dq_in(part, t):
        line = plane[t]
        src = pl.ds(part * two, two)
        dst = pl.ds(pl.multiple_of(line * quarter + part * two, 128), two)
        return copy_to(
            dq_out.at[line, :, src], dq_ref.at[:, dst], d_send.at[part, t], d_recv.at[part, line],
            z * 4 + line, span,
        )

    def one_head(part, b, with_memory):
        tokens = dq_out.shape[0] * dq_out.shape[1]
        here = slice((2 * part + b) * wide, (2 * part + b + 1) * wide)
        query = q_all[:, :, here].reshape(tokens, wide)
        grad = g_all[:, :, here].reshape(tokens, wide)
        key = kv[part, b]
        value = kv[part, 2 + b]
        scores = lax.dot_general(key, query, last, preferred_element_type=F32)
        shifted = jnp.exp2((scores - jnp.max(scores, axis=0, keepdims=True)) * to_exp2)
        probs = shifted * (1.0 / jnp.sum(shifted, axis=0, keepdims=True))
        low = probs.astype(BF)
        probs_grad = lax.dot_general(value, grad, last, preferred_element_type=F32)
        delta = jnp.sum(low.astype(F32) * probs_grad, axis=0, keepdims=True)
        scores_grad = (probs * (probs_grad - delta)).astype(BF)
        dq = lax.dot_general(scores_grad, key, first, preferred_element_type=F32) * scale
        dq_out[:, :, here] = dq.astype(BF).reshape(lines, tokens // lines, wide)
        if with_memory:
            acc[part, b, :, :wide] = jnp.dot(scores_grad, query, preferred_element_type=F32) * scale
            acc[part, b, :, wide:] = jnp.dot(low, grad, preferred_element_type=F32)

    def pair_move(part):
        return copy_to(
            pair_send.at[part], pair_got.at[part], pair_sems.at[part, 0], pair_sems.at[part, 1],
            z_pair * 4 + own_line, span,
        )

    def compute(part):
        @pl.when(span == 1)
        def _():
            for b in range(2):
                one_head(part, b, True)
            pair_send[part] = acc[part, 1 - parity].astype(BF)
            pair_move(part).start()

        @pl.when(span == 0)
        def _():
            for b in range(2):
                one_head(part, b, False)

        for t in range(3):
            dq_move(part, t).start()
        here = pl.ds(part * two, two)
        dst = pl.ds(pl.multiple_of(own_line * quarter + part * two, 128), two)
        dq_ref[:, dst] = dq_out[own_line, :, here]

    def cross_move(part):
        return copy_to(
            cross_send.at[part], cross_got.at[part], cross_sems.at[part, 0], cross_sems.at[part, 1],
            z_cross * 4 + own_line, span,
        )

    def cross(part):
        @pl.when(span == 1)
        def _():
            pair_move(part).wait_recv()
            total = acc[part, parity] + pair_got[part].astype(F32)
            acc[part, parity] = total
            cross_send[part] = total.astype(BF)
            cross_move(part).start()

    def give(part, off):
        p = (in_half + off) % 8
        return copy_to(
            back_send.at[part, p], back.at[part, in_half], b_send.at[part, off], b_recv.at[part, in_half],
            half * 8 + p, other,
        )

    def hand_back(part):
        @pl.when(span == 1)
        def _():
            cross_move(part).wait_recv()
            total = acc[part, parity] + cross_got[part].astype(F32)
            high = total.astype(BF)
            rest = (total - high.astype(F32)).astype(BF)
            mine = picks_ref[:, pl.ds(pl.multiple_of(half * (slots // 2), 128), slots // 2)]
            for i, value in enumerate((high, rest)):
                owned = lax.dot_general(mine, value, first, preferred_element_type=F32)
                back_send[part, :, i] = owned.astype(BF).reshape(n // 2, capacity, two)
            for off in range(n // 2):
                give(part, off).start()

    pack(0)
    send_memory(2)
    send_tokens(1)
    pack(1)
    relay(0)
    send_tokens(2)
    pack(2)
    relay(1)
    for load in own_loads:
        load.wait()
    gathered(0)
    compute(0)
    relay(2)
    gathered(1)
    compute(1)
    cross(0)
    gathered(2)
    compute(2)
    cross(1)
    hand_back(0)
    cross(2)
    hand_back(1)
    hand_back(2)

    @pl.when(span == 1)
    def _():
        dk_ref[...] = jnp.zeros(dk_ref.shape, BF)
        dv_ref[...] = jnp.zeros(dv_ref.shape, BF)

    @pl.when(span == 0)
    def _():
        pool_move().wait_recv()
        matrix = pool_got[...]
        high = matrix.astype(BF)
        rest = (matrix - high.astype(F32)).astype(BF)
        for part in range(parts):
            for p in range(n // 2):
                copy_to(
                    back_send.at[part, p], back.at[part, p], b_send.at[part, p], b_recv.at[part, p], me, other
                ).wait_recv()
                upper = back[part, p, 0]
                lower = back[part, p, 1]
                tokens = jnp.dot(high, lower, preferred_element_type=F32)
                tokens = tokens + jnp.dot(rest, upper, preferred_element_type=F32)
                tokens = (tokens + jnp.dot(high, upper, preferred_element_type=F32)).astype(BF)
                start = ((p % lines) * 2 * parts + 2 * part + p // lines) * wide
                dk_ref[:, start : start + wide] = tokens[:, :wide]
                dv_ref[:, start : start + wide] = tokens[:, wide:]

    for part in range(parts):
        for t in range(3):
            dq_in(part, t).wait_recv()
    for part in range(parts):
        for off in offsets:
            spread(part, off).wait_send()
        for t in range(3):
            exchange(part, t, *queries).wait_send()
            exchange(part, t, *grads).wait_send()
            dq_move(part, t).wait_send()
        along(part, z, z_middle, 0).wait_send()
        along(part, z, z_pair, 1).wait_send()

    @pl.when(middle)
    def _():
        for part in range(parts):
            along(part, z_near, z_pair, 2).wait_send()
            along(part, z_far, z_pair, 3).wait_send()

    @pl.when(span == 1)
    def _():
        pool_move().wait_send()
        for part in range(parts):
            pair_move(part).wait_send()
            cross_move(part).wait_send()
            for off in range(n // 2):
                give(part, off).wait_send()


def settle_kernel(dq_in, dk_in, dv_in, dq_ref, dk_ref, dv_ref, sems):
    moves = [
        pltpu.make_async_copy(src, dst, sems.at[i])
        for i, (src, dst) in enumerate(((dq_in, dq_ref), (dk_in, dk_ref), (dv_in, dv_ref)))
    ]
    for move in moves:
        move.start()
    for move in moves:
        move.wait()


def per_device_fused(query, dout, mem_key, mem_value, keep_count, keep_slot, pool_weight):
    n = 16
    lines = 4
    tokens, width = query.shape[1:]
    capacity = mem_key.shape[1]
    quarter = width // lines
    parts = quarter // (2 * HEAD_DIM)
    vmem = pl.BlockSpec(memory_space=pltpu.VMEM)
    hbm = pl.BlockSpec(memory_space=pltpu.HBM)
    dma = pltpu.SemaphoreType.DMA
    out = jax.ShapeDtypeStruct((tokens, width), BF)
    two = 2 * HEAD_DIM
    owned = (parts, n // 2, 2, capacity, two)
    dq, dk, dv = pl.pallas_call(
        fused_kernel,
        out_shape=(out, out, out),
        in_specs=[hbm] * 7,
        out_specs=(vmem, vmem, vmem),
        scratch_shapes=[
            pltpu.VMEM(keep_count.shape, jnp.int32),
            pltpu.VMEM((keep_slot.shape[2], capacity), jnp.int32),
            pltpu.VMEM((keep_slot.shape[2], capacity), F32),
            pltpu.VMEM((capacity, width), BF),
            pltpu.VMEM((capacity, width), BF),
            pltpu.VMEM((parts, n, capacity, HEAD_DIM), BF),
            pltpu.VMEM((parts, n, capacity, HEAD_DIM), BF),
            pltpu.VMEM((parts, 4, LIVE, HEAD_DIM), BF),
            pltpu.VMEM((lines, tokens, quarter), BF),
            pltpu.VMEM((lines, tokens, quarter), BF),
            pltpu.VMEM((LIVE, n * capacity), BF),
            pltpu.VMEM((lines, tokens, quarter), BF),
            pltpu.VMEM((parts, 2, LIVE, two), F32),
            pltpu.VMEM((parts, LIVE, two), BF),
            pltpu.VMEM((parts, LIVE, two), BF),
            pltpu.VMEM((parts, LIVE, two), BF),
            pltpu.VMEM((parts, LIVE, two), BF),
            pltpu.VMEM(owned, BF),
            pltpu.VMEM(owned, BF),
            pltpu.VMEM((tokens, capacity), F32),
            pltpu.VMEM((tokens, capacity), F32),
            dma((7,)), dma((parts, n)), dma((parts, n)), dma((parts, 4)), dma((parts, 4)),
            dma((parts, 3)), dma((parts, lines)), dma((parts, 3)), dma((parts, lines)),
            dma((parts, 3)), dma((parts, lines)),
            dma((parts, 2)), dma((parts, 2)), dma((parts, n // 2)), dma((parts, n // 2)), dma, dma,
        ],
        compiler_params=pltpu.CompilerParams(
            collective_id=0, has_side_effects=True, vmem_limit_bytes=32 << 20
        ),
    )(
        *(
            pltpu.with_memory_space_constraint(value, pltpu.HBM)
            for value in (
                query[0], dout[0], mem_key[0], mem_value[0], keep_count, keep_slot[0].T, pool_weight[0].T,
            )
        )
    )
    any_space = pl.BlockSpec(memory_space=pl.ANY)
    dq, dk, dv = pl.pallas_call(
        settle_kernel,
        out_shape=(out, out, out),
        in_specs=[any_space] * 3,
        out_specs=(any_space,) * 3,
        scratch_shapes=[dma((3,))],
        compiler_params=pltpu.CompilerParams(vmem_limit_bytes=32 << 20),
    )(dq, dk, dv)
    return dq[None], dk[None], dv[None]


def solution(mesh):
    fused = mesh.shape["seq"] == 16 and mesh.shape["span"] == 2
    return jax.shard_map(
        per_device_fused if fused else per_device,
        mesh=mesh,
        in_specs=(
            P("span", "seq", None),
            P("span", "seq", None),
            P("span", "seq", None),
            P("span", "seq", None),
            P("span", None),
            P("span", "seq", None),
            P("span", "seq", None),
        ),
        out_specs=(P("span", "seq", None), P("span", "seq", None), P("span", "seq", None)),
        check_vma=False,
    )
```

```python
import math

import jax
import jax.numpy as jnp
from jax import lax
from jax.experimental import pallas as pl
from jax.experimental.pallas import tpu as pltpu
from jax.sharding import PartitionSpec as P

HEAD_DIM = 128
LIVE = 256
BF = jnp.bfloat16
F32 = jnp.float32


def passed_along(block, axis, distance):
    devices = range(lax.axis_size(axis))
    route = [(i - distance, i) for i in devices if i - distance in devices]
    return lax.ppermute(block, axis, route)


def head_backward(query_head, grad_head, key_head, value_head, live_mask, block_rows):
    score_scale = key_head.shape[1] ** (-0.5)
    head_width = query_head.shape[1]
    blocks = query_head.shape[0] // block_rows
    query_blocks = query_head.reshape(blocks, block_rows, head_width)
    grad_blocks = grad_head.reshape(blocks, block_rows, head_width)

    def visit_block(totals, inputs):
        key_grad, value_grad = totals
        query_block, grad_block = inputs
        scores = jnp.dot(query_block, key_head.T, preferred_element_type=jnp.float32) * score_scale
        scores = jnp.where(live_mask[None, :], scores, -jnp.inf)
        shifted = jnp.exp(scores - jnp.max(scores, axis=1, keepdims=True))
        probs_full = shifted / jnp.sum(shifted, axis=1, keepdims=True)
        probs_low = probs_full.astype(jnp.bfloat16)
        attn_out = jnp.dot(probs_low, value_head, preferred_element_type=jnp.float32)
        deltas = jnp.sum(grad_block.astype(jnp.float32) * attn_out, axis=1, keepdims=True)
        probs_grad = jnp.dot(grad_block, value_head.T, preferred_element_type=jnp.float32)
        scores_grad = (probs_full * (probs_grad - deltas)).astype(jnp.bfloat16)
        query_grad = (
            jnp.dot(scores_grad, key_head, preferred_element_type=jnp.float32) * score_scale
        ).astype(jnp.bfloat16)
        key_grad = (
            key_grad
            + lax.dot_general(
                scores_grad,
                query_block,
                (((0,), (0,)), ((), ())),
                preferred_element_type=jnp.float32,
            )
            * score_scale
        )
        value_grad = value_grad + lax.dot_general(
            probs_low, grad_block, (((0,), (0,)), ((), ())), preferred_element_type=jnp.float32
        )
        return ((key_grad, value_grad), query_grad)

    empty_grad = jnp.zeros(key_head.shape, jnp.float32)
    (key_grad, value_grad), query_grad = lax.scan(
        visit_block, (empty_grad, empty_grad), (query_blocks, grad_blocks)
    )
    return (query_grad.reshape(-1, head_width), key_grad, value_grad)


def owner_rows(key_parts, value_parts, token_parts, groups, row_count):
    got_key, got_value = (
        lax.all_to_all(key_parts, "seq", split_axis=0, concat_axis=0, tiled=True),
        lax.all_to_all(value_parts, "seq", split_axis=0, concat_axis=0, tiled=True),
    )

    def fold_parts(values):
        shaped = values.reshape(token_parts, groups, row_count, values.shape[2], values.shape[3])
        summed = jnp.sum(shaped, axis=0)
        return summed.transpose(1, 0, 2, 3).reshape(row_count, -1)

    return (fold_parts(got_key), fold_parts(got_value))


def pool_matrix(slots, weights, local_tokens):
    positions = jnp.arange(local_tokens)
    onehot = (slots[:, :, None] == positions[None, None, :]).astype(jnp.float32)
    return jnp.einsum("cjt,cj->tc", onehot, weights, precision=lax.Precision.HIGHEST)


def apply_pool(matrix, key_rows, value_rows):
    stacked = jnp.concatenate([key_rows, value_rows], axis=1)
    return jnp.dot(
        matrix, stacked, precision=lax.Precision.HIGHEST, preferred_element_type=jnp.float32
    )


def per_device(query, dout, mem_key, mem_value, keep_count, keep_slot, pool_weight):
    devices = lax.axis_size("seq")
    head_width = HEAD_DIM
    head_count = query.shape[2] // head_width
    groups = math.gcd(head_count, devices)
    token_parts = devices // groups
    group_heads = head_count // groups
    local_tokens = query.shape[1]
    part_rows = local_tokens // token_parts
    capacity = mem_key.shape[1]
    owner_counts = keep_count[0]

    def token_layout(values):
        shaped = values.reshape(token_parts, part_rows, groups, group_heads, head_width)
        return shaped.transpose(0, 2, 1, 3, 4).reshape(devices, part_rows, group_heads, head_width)

    def memory_layout(values):
        row_count = values.shape[0]
        shaped = values.reshape(row_count, groups, group_heads, head_width).transpose(1, 0, 2, 3)
        spread = jnp.broadcast_to(shaped[None], (token_parts,) + shaped.shape)
        return spread.reshape(devices, row_count, group_heads, head_width)

    slot_index = jnp.arange(devices * capacity)
    live_mask = slot_index % capacity < jnp.repeat(owner_counts, capacity)
    key_used, value_used = (mem_key[0], mem_value[0])
    query_rows = lax.all_to_all(
        token_layout(query[0]), "seq", split_axis=0, concat_axis=0, tiled=True
    )
    grad_rows = lax.all_to_all(
        token_layout(dout[0]), "seq", split_axis=0, concat_axis=0, tiled=True
    )
    key_rows = lax.all_to_all(
        memory_layout(key_used), "seq", split_axis=0, concat_axis=0, tiled=True
    )
    value_rows = lax.all_to_all(
        memory_layout(value_used), "seq", split_axis=0, concat_axis=0, tiled=True
    )
    item_heads = query_rows.shape[2]
    row_count = key_rows.shape[1]
    query_total = devices * part_rows
    block_rows = 512
    query_flat = jnp.moveaxis(query_rows.reshape(query_total, item_heads, head_width), 1, 0)
    grad_flat = jnp.moveaxis(grad_rows.reshape(query_total, item_heads, head_width), 1, 0)
    key_flat = jnp.moveaxis(key_rows.reshape(devices * row_count, item_heads, head_width), 1, 0)
    value_flat = jnp.moveaxis(value_rows.reshape(devices * row_count, item_heads, head_width), 1, 0)

    def one_head(pieces):
        return head_backward(pieces[0], pieces[1], pieces[2], pieces[3], live_mask, block_rows)

    query_grad, key_grad, value_grad = lax.map(
        one_head, (query_flat, grad_flat, key_flat, value_flat)
    )
    query_back = jnp.moveaxis(query_grad, 0, 1).reshape(devices, part_rows, item_heads, head_width)
    key_back = jnp.moveaxis(key_grad, 0, 1).reshape(devices, row_count, item_heads, head_width)
    value_back = jnp.moveaxis(value_grad, 0, 1).reshape(devices, row_count, item_heads, head_width)
    returned = lax.all_to_all(query_back, "seq", split_axis=0, concat_axis=0, tiled=True)
    returned = returned.reshape(token_parts, groups, part_rows, group_heads, head_width).transpose(
        0, 2, 1, 3, 4
    )
    dquery = returned.reshape(1, local_tokens, groups * group_heads * head_width)
    matrix = pool_matrix(keep_slot[0], pool_weight[0], local_tokens)
    key_rows, value_rows = owner_rows(key_back, value_back, token_parts, groups, capacity)
    local_grad = apply_pool(matrix, key_rows, value_rows).astype(jnp.bfloat16)
    tokens_grad = passed_along(local_grad, "span", -1)
    feature_width = groups * group_heads * head_width
    dkey_tok = tokens_grad[None, :, :feature_width]
    dvalue_tok = tokens_grad[None, :, feature_width:]
    return (dquery, dkey_tok, dvalue_tok)


def copy_to(src, dst, send_sem, recv_sem, seq, span):
    return pltpu.make_async_remote_copy(
        src_ref=src,
        dst_ref=dst,
        send_sem=send_sem,
        recv_sem=recv_sem,
        device_id={"seq": seq, "span": span},
        device_id_type=pl.DeviceIdType.MESH,
    )


def fused_kernel(
    q_hbm, g_hbm, k_hbm, v_hbm, count_hbm, slot_hbm, weight_hbm,
    dq_ref, dk_ref, dv_ref,
    count_ref, slot_ref, weight_ref, k_ref, v_ref, kvin, rows, kv, q_all, g_all, picks_ref, mine_ref, dq_out,
    acc, pair_send, pair_got, cross_send, cross_got, back_send, back, pool_send, pool_got,
    in_sem, a_send, a_recv, z_send, z_recv, q_send, q_recv, g_send, g_recv, d_send, d_recv,
    pair_sems, cross_sems, b_send, b_recv, p_send, p_recv,
):
    n = 16
    lines = 4
    parts = kv.shape[0]
    wide = HEAD_DIM
    two = 2 * wide
    quarter = q_all.shape[2]
    chunks = tuple((2 * part, 2 * part + 2) for part in range(parts - 1))
    chunks = chunks + ((2 * parts - 2, 2 * parts - 1), (2 * parts - 1, 2 * parts))
    me = lax.axis_index("seq")
    span = lax.axis_index("span")
    other = 1 - span
    capacity = k_ref.shape[0]
    z, y, x = me // 4, (me // 2) % 2, me % 2
    own_line = me % 4
    x_line = own_line + 1 - 2 * x
    y_line = own_line + 2 - 4 * y
    d_line = 3 - own_line
    plane = (x_line, y_line, d_line)
    parity = z % 2
    half = z // 2
    in_half = me % 8
    middle = (z == 1) | (z == 2)
    z_pair = z + 1 - 2 * parity
    z_middle = 2 - half
    z_far = 3 - 3 * half
    z_near = 2 - half
    z_cross = (z + 2) % 4
    scale = HEAD_DIM ** (-0.5)
    to_exp2 = scale * math.log2(math.e)
    last = (((1,), (1,)), ((), ()))
    first = (((0,), (0,)), ((), ()))

    loads = [
        pltpu.make_async_copy(k_hbm, k_ref, in_sem.at[0]),
        pltpu.make_async_copy(v_hbm, v_ref, in_sem.at[1]),
    ]
    own_quarter = pl.ds(pl.multiple_of(own_line * quarter, 128), quarter)
    own_loads = [
        pltpu.make_async_copy(q_hbm.at[:, own_quarter], q_all.at[own_line], in_sem.at[2]),
        pltpu.make_async_copy(g_hbm.at[:, own_quarter], g_all.at[own_line], in_sem.at[3]),
    ]
    small_loads = [
        pltpu.make_async_copy(count_hbm, count_ref, in_sem.at[4]),
        pltpu.make_async_copy(slot_hbm, slot_ref, in_sem.at[5]),
        pltpu.make_async_copy(weight_hbm, weight_ref, in_sem.at[6]),
    ]
    for load in loads + small_loads + own_loads:
        load.start()
    barrier = pltpu.get_barrier_semaphore()
    for off in range(1, n):
        pl.semaphore_signal(
            barrier, inc=1, device_id={"seq": (me + off) % n, "span": span},
            device_id_type=pl.DeviceIdType.MESH,
        )
    for off in range(n // 2):
        pl.semaphore_signal(
            barrier, inc=1, device_id={"seq": half * 8 + (in_half + off) % 8, "span": other},
            device_id_type=pl.DeviceIdType.MESH,
        )
    for load in loads + small_loads:
        load.wait()
    for p in range(n):
        source = k_ref if p < n // 2 else v_ref
        for part in range(parts):
            start = ((p % lines) * 2 * parts + 2 * part + (p // lines) % 2) * wide
            kvin[part, p] = source[:, start : start + wide]
    pl.semaphore_wait(barrier, n - 1 + n // 2)

    def spread(part, off):
        p = (me + off) % n
        return copy_to(kvin.at[part, p], rows.at[part, me], a_send.at[part, off], a_recv.at[part, me], p, span)

    def spread_in(part, off):
        p = (me + off) % n
        return copy_to(kvin.at[part, p], rows.at[part, p], a_send.at[part, off], a_recv.at[part, p], p, span)

    offsets = (15, 1, 14, 2, 13, 3, 12, 4, 11, 5, 10, 6, 9, 7, 8)

    def send_memory(part):
        for off in offsets:
            spread(part, off).start()
        rows[part, me] = kvin[part, me]

    def exchange(part, t, whole, held, send_sem, recv_sem):
        line = plane[t]
        src = pl.ds(pl.multiple_of(line * quarter + part * two, 128), two)
        dst = pl.ds(part * two, two)
        return copy_to(
            whole.at[:, src], held.at[own_line, :, dst], send_sem.at[part, t], recv_sem.at[part, own_line],
            z * 4 + line, span,
        )

    def exchange_in(part, t, whole, held, send_sem, recv_sem):
        line = plane[t]
        dst = pl.ds(part * two, two)
        return copy_to(
            whole.at[:, dst], held.at[line, :, dst], send_sem.at[part, t], recv_sem.at[part, line],
            z * 4 + line, span,
        )

    queries = (q_hbm, q_all, q_send, q_recv)
    grads = (g_hbm, g_all, g_send, g_recv)
    def send_tokens(part):
        for t in range(3):
            exchange(part, t, *queries).start()
            exchange(part, t, *grads).start()

    send_memory(0)
    send_tokens(0)
    send_memory(1)

    def pool_move():
        return copy_to(pool_send, pool_got, p_send, p_recv, me, other)

    @pl.when(span == 1)
    def _():
        spots = lax.broadcasted_iota(jnp.int32, pool_send.shape, 0)
        total = jnp.zeros(pool_send.shape, F32)
        for j in range(slot_ref.shape[0]):
            total = total + jnp.where(spots == slot_ref[j : j + 1, :], weight_ref[j : j + 1, :], 0.0)
        pool_send[...] = total
        pool_move().start()

    slots = n * capacity
    counts = jnp.broadcast_to(count_ref[...], (8, n)).astype(F32).astype(BF)
    owner = lax.broadcasted_iota(jnp.int32, (n, slots), 1)
    below = lax.broadcasted_iota(jnp.int32, (n, slots), 0) * capacity
    ahead = jnp.where(owner >= below + capacity, 1.0, 0.0).astype(BF)
    inside = jnp.where((owner >= below) & (owner < below + capacity), 1.0, 0.0).astype(BF)
    position = jnp.where((owner >= below) & (owner < below + capacity), owner - below, 0)
    position = jnp.sum(position.astype(F32), axis=0, keepdims=True)
    offset = jnp.dot(counts, ahead, preferred_element_type=F32)[:1]
    length = jnp.dot(counts, inside, preferred_element_type=F32)[:1]
    place = jnp.where(position < length, offset + position, -1.0).astype(jnp.int32)
    picks = lax.broadcasted_iota(jnp.int32, (LIVE, slots), 0) == place
    picks_ref[...] = jnp.where(picks, 1.0, 0.0).astype(BF)

    @pl.when(span == 1)
    def _():
        mine = picks_ref[:, pl.ds(pl.multiple_of(half * (slots // 2), 128), slots // 2)]
        unit = lax.broadcasted_iota(jnp.int32, (LIVE, LIVE), 0) == lax.broadcasted_iota(jnp.int32, (LIVE, LIVE), 1)
        unit = jnp.where(unit, 1.0, 0.0).astype(BF)
        mine_ref[...] = lax.dot_general(mine, unit, first, preferred_element_type=F32).astype(BF)


    def along(part, source, target, k):
        block = kv.at[part, source]
        return copy_to(block, block, z_send.at[part, k], z_recv.at[part, source], target * 4 + own_line, span)

    def pack(part):
        for off in offsets:
            spread_in(part, off).wait_recv()
        packed = jnp.dot(picks_ref[...], rows[part].reshape(slots, wide), preferred_element_type=F32)
        kv[part, z] = packed.astype(BF)
        along(part, z, z_middle, 0).start()
        along(part, z, z_pair, 1).start()

    def relay(part):
        @pl.when(middle)
        def _():
            along(part, z_near, z_pair, 2).wait_recv()
            along(part, z_near, z_pair, 2).start()
            along(part, z_far, z_pair, 3).wait_recv()
            along(part, z_far, z_pair, 3).start()

    def gathered(part):
        along(part, z_pair, z_pair, 1).wait_recv()

        @pl.when(jnp.logical_not(middle))
        def _():
            along(part, z_near, z_pair, 2).wait_recv()
            along(part, z_far, z_pair, 3).wait_recv()

        for t in range(3):
            exchange_in(part, t, *queries).wait_recv()
            exchange_in(part, t, *grads).wait_recv()

    def dq_move(part, t):
        line = plane[t]
        src = pl.ds(part * two, two)
        dst = pl.ds(pl.multiple_of(own_line * quarter + part * two, 128), two)
        return copy_to(
            dq_out.at[line, :, src], dq_ref.at[:, dst], d_send.at[part, t], d_recv.at[part, own_line],
            z * 4 + line, span,
        )

    def dq_in(part, t):
        line = plane[t]
        src = pl.ds(part * two, two)
        dst = pl.ds(pl.multiple_of(line * quarter + part * two, 128), two)
        return copy_to(
            dq_out.at[line, :, src], dq_ref.at[:, dst], d_send.at[part, t], d_recv.at[part, line],
            z * 4 + line, span,
        )

    def one_head(part, b, with_memory):
        tokens = dq_out.shape[0] * dq_out.shape[1]
        here = slice((2 * part + b) * wide, (2 * part + b + 1) * wide)
        query = q_all[:, :, here].reshape(tokens, wide)
        grad = g_all[:, :, here].reshape(tokens, wide)
        key = kv[part, b]
        value = kv[part, 2 + b]
        scores = lax.dot_general(key, query, last, preferred_element_type=F32)
        shifted = jnp.exp2((scores - jnp.max(scores, axis=0, keepdims=True)) * to_exp2)
        probs = shifted * (1.0 / jnp.sum(shifted, axis=0, keepdims=True))
        low = probs.astype(BF)
        probs_grad = lax.dot_general(value, grad, last, preferred_element_type=F32)
        delta = jnp.sum(low.astype(F32) * probs_grad, axis=0, keepdims=True)
        scores_grad = (probs * (probs_grad - delta)).astype(BF)
        dq = lax.dot_general(scores_grad, key, first, preferred_element_type=F32) * scale
        dq_out[:, :, here] = dq.astype(BF).reshape(lines, tokens // lines, wide)
        if with_memory:
            acc[0, 2 * part + b] = jnp.dot(scores_grad, query, preferred_element_type=F32) * scale
            acc[1, 2 * part + b] = jnp.dot(low, grad, preferred_element_type=F32)

    def pair_move(chunk):
        heads = slice(*chunks[chunk])
        return copy_to(
            pair_send.at[heads], pair_got.at[heads], pair_sems.at[chunk, 0], pair_sems.at[chunk, 1],
            z_pair * 4 + own_line, span,
        )

    def compute(part):
        @pl.when(span == 1)
        def _():
            for b in range(2):
                one_head(part, b, True)
                for chunk, (lo, hi) in enumerate(chunks):
                    if hi == 2 * part + b + 1:
                        pair_send[lo:hi] = acc[1 - parity, lo:hi].astype(BF)
                        pair_move(chunk).start()

        @pl.when(span == 0)
        def _():
            for b in range(2):
                one_head(part, b, False)

    def send_dq(part):
        for t in range(3):
            dq_move(part, t).start()
        here = pl.ds(part * two, two)
        dst = pl.ds(pl.multiple_of(own_line * quarter + part * two, 128), two)
        dq_ref[:, dst] = dq_out[own_line, :, here]

    def cross_move(chunk):
        heads = slice(*chunks[chunk])
        return copy_to(
            cross_send.at[heads], cross_got.at[heads], cross_sems.at[chunk, 0], cross_sems.at[chunk, 1],
            z_cross * 4 + own_line, span,
        )

    def cross(chunk):
        lo, hi = chunks[chunk]

        @pl.when(span == 1)
        def _():
            pair_move(chunk).wait_recv()
            total = acc[parity, lo:hi] + pair_got[lo:hi].astype(F32)
            acc[parity, lo:hi] = total
            cross_send[lo:hi] = total.astype(BF)
            cross_move(chunk).start()

    def give(chunk, off):
        p = (in_half + off) % 8
        lo, hi = chunks[chunk]
        heads = pl.ds(lo, hi - lo)
        return copy_to(
            back_send.at[p, heads], back.at[in_half, heads], b_send.at[chunk, off], b_recv.at[chunk, in_half],
            half * 8 + p, other,
        )

    def hand_back(chunk):
        @pl.when(span == 1)
        def _():
            cross_move(chunk).wait_recv()
            for head in range(*chunks[chunk]):
                total = acc[parity, head] + cross_got[head].astype(F32)
                high = total.astype(BF)
                rest = (total - high.astype(F32)).astype(BF)
                both = jnp.concatenate([high, rest], axis=1)
                owned = jnp.dot(mine_ref[...], both, preferred_element_type=F32).astype(BF)
                back_send[:, head, 0] = owned[:, :wide].reshape(n // 2, capacity, wide)
                back_send[:, head, 1] = owned[:, wide:].reshape(n // 2, capacity, wide)
            for off in range(n // 2):
                give(chunk, off).start()

    pack(0)
    send_memory(2)
    send_tokens(1)
    pack(1)
    relay(0)
    send_tokens(2)
    pack(2)
    relay(1)
    for load in own_loads:
        load.wait()
    gathered(0)
    compute(0)
    send_dq(0)
    relay(2)
    gathered(1)
    compute(1)
    send_dq(1)
    cross(0)
    cross(1)
    gathered(2)
    compute(2)
    hand_back(0)
    cross(2)
    cross(3)
    hand_back(1)
    send_dq(2)
    hand_back(2)
    hand_back(3)

    @pl.when(span == 1)
    def _():
        dk_ref[...] = jnp.zeros(dk_ref.shape, BF)
        dv_ref[...] = jnp.zeros(dv_ref.shape, BF)

    @pl.when(span == 0)
    def _():
        pool_move().wait_recv()
        matrix = pool_got[...]
        high = matrix.astype(BF)
        rest = (matrix - high.astype(F32)).astype(BF)
        stacked = jnp.concatenate([high, rest], axis=0)
        for chunk, (lo, hi) in enumerate(chunks):
            heads = pl.ds(lo, hi - lo)
            for p in range(n // 2):
                copy_to(
                    back_send.at[p, heads], back.at[p, heads], b_send.at[chunk, p], b_recv.at[chunk, p], me, other
                ).wait_recv()
            for head in range(lo, hi):
                for kind, result in enumerate((dk_ref, dv_ref)):
                    upper = jnp.concatenate([back[kind * lines + i, head, 0] for i in range(lines)], axis=1)
                    lower = jnp.concatenate([back[kind * lines + i, head, 1] for i in range(lines)], axis=1)
                    tokens = jnp.dot(stacked, upper, preferred_element_type=F32)
                    tokens = tokens[: matrix.shape[0]] + tokens[matrix.shape[0] :]
                    tokens = tokens + jnp.dot(high, lower, preferred_element_type=F32)
                    tokens = tokens.astype(BF)
                    for i in range(lines):
                        start = (i * 2 * parts + head) * wide
                        result[:, start : start + wide] = tokens[:, i * wide : (i + 1) * wide]

    for part in range(parts):
        for t in range(3):
            dq_in(part, t).wait_recv()
    for part in range(parts):
        for off in offsets:
            spread(part, off).wait_send()
        for t in range(3):
            exchange(part, t, *queries).wait_send()
            exchange(part, t, *grads).wait_send()
            dq_move(part, t).wait_send()
        along(part, z, z_middle, 0).wait_send()
        along(part, z, z_pair, 1).wait_send()

    @pl.when(middle)
    def _():
        for part in range(parts):
            along(part, z_near, z_pair, 2).wait_send()
            along(part, z_far, z_pair, 3).wait_send()

    @pl.when(span == 1)
    def _():
        pool_move().wait_send()
        for chunk in range(len(chunks)):
            pair_move(chunk).wait_send()
            cross_move(chunk).wait_send()
            for off in range(n // 2):
                give(chunk, off).wait_send()


def settle_kernel(dq_in, dk_in, dv_in, dq_ref, dk_ref, dv_ref, sems):
    moves = [
        pltpu.make_async_copy(src, dst, sems.at[i])
        for i, (src, dst) in enumerate(((dq_in, dq_ref), (dk_in, dk_ref), (dv_in, dv_ref)))
    ]
    for move in moves:
        move.start()
    for move in moves:
        move.wait()


def per_device_fused(query, dout, mem_key, mem_value, keep_count, keep_slot, pool_weight):
    n = 16
    lines = 4
    tokens, width = query.shape[1:]
    capacity = mem_key.shape[1]
    quarter = width // lines
    parts = quarter // (2 * HEAD_DIM)
    vmem = pl.BlockSpec(memory_space=pltpu.VMEM)
    hbm = pl.BlockSpec(memory_space=pltpu.HBM)
    dma = pltpu.SemaphoreType.DMA
    out = jax.ShapeDtypeStruct((tokens, width), BF)
    heads = 2 * parts
    owned = (n // 2, heads, 2, capacity, HEAD_DIM)
    dq, dk, dv = pl.pallas_call(
        fused_kernel,
        out_shape=(out, out, out),
        in_specs=[hbm] * 7,
        out_specs=(vmem, vmem, vmem),
        scratch_shapes=[
            pltpu.VMEM(keep_count.shape, jnp.int32),
            pltpu.VMEM((keep_slot.shape[2], capacity), jnp.int32),
            pltpu.VMEM((keep_slot.shape[2], capacity), F32),
            pltpu.VMEM((capacity, width), BF),
            pltpu.VMEM((capacity, width), BF),
            pltpu.VMEM((parts, n, capacity, HEAD_DIM), BF),
            pltpu.VMEM((parts, n, capacity, HEAD_DIM), BF),
            pltpu.VMEM((parts, 4, LIVE, HEAD_DIM), BF),
            pltpu.VMEM((lines, tokens, quarter), BF),
            pltpu.VMEM((lines, tokens, quarter), BF),
            pltpu.VMEM((LIVE, n * capacity), BF),
            pltpu.VMEM((n // 2 * capacity, LIVE), BF),
            pltpu.VMEM((lines, tokens, quarter), BF),
            pltpu.VMEM((2, heads, LIVE, HEAD_DIM), F32),
            pltpu.VMEM((heads, LIVE, HEAD_DIM), BF),
            pltpu.VMEM((heads, LIVE, HEAD_DIM), BF),
            pltpu.VMEM((heads, LIVE, HEAD_DIM), BF),
            pltpu.VMEM((heads, LIVE, HEAD_DIM), BF),
            pltpu.VMEM(owned, BF),
            pltpu.VMEM(owned, BF),
            pltpu.VMEM((tokens, capacity), F32),
            pltpu.VMEM((tokens, capacity), F32),
            dma((7,)), dma((parts, n)), dma((parts, n)), dma((parts, 4)), dma((parts, 4)),
            dma((parts, 3)), dma((parts, lines)), dma((parts, 3)), dma((parts, lines)),
            dma((parts, 3)), dma((parts, lines)),
            dma((parts + 1, 2)), dma((parts + 1, 2)), dma((parts + 1, n // 2)), dma((parts + 1, n // 2)), dma, dma,
        ],
        compiler_params=pltpu.CompilerParams(
            collective_id=0, has_side_effects=True, vmem_limit_bytes=32 << 20
        ),
    )(
        *(
            pltpu.with_memory_space_constraint(value, pltpu.HBM)
            for value in (
                query[0], dout[0], mem_key[0], mem_value[0], keep_count, keep_slot[0].T, pool_weight[0].T,
            )
        )
    )
    any_space = pl.BlockSpec(memory_space=pl.ANY)
    dq, dk, dv = pl.pallas_call(
        settle_kernel,
        out_shape=(out, out, out),
        in_specs=[any_space] * 3,
        out_specs=(any_space,) * 3,
        scratch_shapes=[dma((3,))],
        compiler_params=pltpu.CompilerParams(vmem_limit_bytes=32 << 20),
    )(dq, dk, dv)
    return dq[None], dk[None], dv[None]


def solution(mesh):
    fused = mesh.shape["seq"] == 16 and mesh.shape["span"] == 2
    return jax.shard_map(
        per_device_fused if fused else per_device,
        mesh=mesh,
        in_specs=(
            P("span", "seq", None),
            P("span", "seq", None),
            P("span", "seq", None),
            P("span", "seq", None),
            P("span", None),
            P("span", "seq", None),
            P("span", "seq", None),
        ),
        out_specs=(P("span", "seq", None), P("span", "seq", None), P("span", "seq", None)),
        check_vma=False,
    )
```

```python
import math

import jax
import jax.numpy as jnp
from jax import lax
from jax.experimental import pallas as pl
from jax.experimental.pallas import tpu as pltpu
from jax.sharding import PartitionSpec as P

HEAD_DIM = 128
LIVE = 256
BF = jnp.bfloat16
F32 = jnp.float32


def passed_along(block, axis, distance):
    devices = range(lax.axis_size(axis))
    route = [(i - distance, i) for i in devices if i - distance in devices]
    return lax.ppermute(block, axis, route)


def head_backward(query_head, grad_head, key_head, value_head, live_mask, block_rows):
    score_scale = key_head.shape[1] ** (-0.5)
    head_width = query_head.shape[1]
    blocks = query_head.shape[0] // block_rows
    query_blocks = query_head.reshape(blocks, block_rows, head_width)
    grad_blocks = grad_head.reshape(blocks, block_rows, head_width)

    def visit_block(totals, inputs):
        key_grad, value_grad = totals
        query_block, grad_block = inputs
        scores = jnp.dot(query_block, key_head.T, preferred_element_type=jnp.float32) * score_scale
        scores = jnp.where(live_mask[None, :], scores, -jnp.inf)
        shifted = jnp.exp(scores - jnp.max(scores, axis=1, keepdims=True))
        probs_full = shifted / jnp.sum(shifted, axis=1, keepdims=True)
        probs_low = probs_full.astype(jnp.bfloat16)
        attn_out = jnp.dot(probs_low, value_head, preferred_element_type=jnp.float32)
        deltas = jnp.sum(grad_block.astype(jnp.float32) * attn_out, axis=1, keepdims=True)
        probs_grad = jnp.dot(grad_block, value_head.T, preferred_element_type=jnp.float32)
        scores_grad = (probs_full * (probs_grad - deltas)).astype(jnp.bfloat16)
        query_grad = (
            jnp.dot(scores_grad, key_head, preferred_element_type=jnp.float32) * score_scale
        ).astype(jnp.bfloat16)
        key_grad = (
            key_grad
            + lax.dot_general(
                scores_grad,
                query_block,
                (((0,), (0,)), ((), ())),
                preferred_element_type=jnp.float32,
            )
            * score_scale
        )
        value_grad = value_grad + lax.dot_general(
            probs_low, grad_block, (((0,), (0,)), ((), ())), preferred_element_type=jnp.float32
        )
        return ((key_grad, value_grad), query_grad)

    empty_grad = jnp.zeros(key_head.shape, jnp.float32)
    (key_grad, value_grad), query_grad = lax.scan(
        visit_block, (empty_grad, empty_grad), (query_blocks, grad_blocks)
    )
    return (query_grad.reshape(-1, head_width), key_grad, value_grad)


def owner_rows(key_parts, value_parts, token_parts, groups, row_count):
    got_key, got_value = (
        lax.all_to_all(key_parts, "seq", split_axis=0, concat_axis=0, tiled=True),
        lax.all_to_all(value_parts, "seq", split_axis=0, concat_axis=0, tiled=True),
    )

    def fold_parts(values):
        shaped = values.reshape(token_parts, groups, row_count, values.shape[2], values.shape[3])
        summed = jnp.sum(shaped, axis=0)
        return summed.transpose(1, 0, 2, 3).reshape(row_count, -1)

    return (fold_parts(got_key), fold_parts(got_value))


def pool_matrix(slots, weights, local_tokens):
    positions = jnp.arange(local_tokens)
    onehot = (slots[:, :, None] == positions[None, None, :]).astype(jnp.float32)
    return jnp.einsum("cjt,cj->tc", onehot, weights, precision=lax.Precision.HIGHEST)


def apply_pool(matrix, key_rows, value_rows):
    stacked = jnp.concatenate([key_rows, value_rows], axis=1)
    return jnp.dot(
        matrix, stacked, precision=lax.Precision.HIGHEST, preferred_element_type=jnp.float32
    )


def per_device(query, dout, mem_key, mem_value, keep_count, keep_slot, pool_weight):
    devices = lax.axis_size("seq")
    head_width = HEAD_DIM
    head_count = query.shape[2] // head_width
    groups = math.gcd(head_count, devices)
    token_parts = devices // groups
    group_heads = head_count // groups
    local_tokens = query.shape[1]
    part_rows = local_tokens // token_parts
    capacity = mem_key.shape[1]
    owner_counts = keep_count[0]

    def token_layout(values):
        shaped = values.reshape(token_parts, part_rows, groups, group_heads, head_width)
        return shaped.transpose(0, 2, 1, 3, 4).reshape(devices, part_rows, group_heads, head_width)

    def memory_layout(values):
        row_count = values.shape[0]
        shaped = values.reshape(row_count, groups, group_heads, head_width).transpose(1, 0, 2, 3)
        spread = jnp.broadcast_to(shaped[None], (token_parts,) + shaped.shape)
        return spread.reshape(devices, row_count, group_heads, head_width)

    slot_index = jnp.arange(devices * capacity)
    live_mask = slot_index % capacity < jnp.repeat(owner_counts, capacity)
    key_used, value_used = (mem_key[0], mem_value[0])
    query_rows = lax.all_to_all(
        token_layout(query[0]), "seq", split_axis=0, concat_axis=0, tiled=True
    )
    grad_rows = lax.all_to_all(
        token_layout(dout[0]), "seq", split_axis=0, concat_axis=0, tiled=True
    )
    key_rows = lax.all_to_all(
        memory_layout(key_used), "seq", split_axis=0, concat_axis=0, tiled=True
    )
    value_rows = lax.all_to_all(
        memory_layout(value_used), "seq", split_axis=0, concat_axis=0, tiled=True
    )
    item_heads = query_rows.shape[2]
    row_count = key_rows.shape[1]
    query_total = devices * part_rows
    block_rows = 512
    query_flat = jnp.moveaxis(query_rows.reshape(query_total, item_heads, head_width), 1, 0)
    grad_flat = jnp.moveaxis(grad_rows.reshape(query_total, item_heads, head_width), 1, 0)
    key_flat = jnp.moveaxis(key_rows.reshape(devices * row_count, item_heads, head_width), 1, 0)
    value_flat = jnp.moveaxis(value_rows.reshape(devices * row_count, item_heads, head_width), 1, 0)

    def one_head(pieces):
        return head_backward(pieces[0], pieces[1], pieces[2], pieces[3], live_mask, block_rows)

    query_grad, key_grad, value_grad = lax.map(
        one_head, (query_flat, grad_flat, key_flat, value_flat)
    )
    query_back = jnp.moveaxis(query_grad, 0, 1).reshape(devices, part_rows, item_heads, head_width)
    key_back = jnp.moveaxis(key_grad, 0, 1).reshape(devices, row_count, item_heads, head_width)
    value_back = jnp.moveaxis(value_grad, 0, 1).reshape(devices, row_count, item_heads, head_width)
    returned = lax.all_to_all(query_back, "seq", split_axis=0, concat_axis=0, tiled=True)
    returned = returned.reshape(token_parts, groups, part_rows, group_heads, head_width).transpose(
        0, 2, 1, 3, 4
    )
    dquery = returned.reshape(1, local_tokens, groups * group_heads * head_width)
    matrix = pool_matrix(keep_slot[0], pool_weight[0], local_tokens)
    key_rows, value_rows = owner_rows(key_back, value_back, token_parts, groups, capacity)
    local_grad = apply_pool(matrix, key_rows, value_rows).astype(jnp.bfloat16)
    tokens_grad = passed_along(local_grad, "span", -1)
    feature_width = groups * group_heads * head_width
    dkey_tok = tokens_grad[None, :, :feature_width]
    dvalue_tok = tokens_grad[None, :, feature_width:]
    return (dquery, dkey_tok, dvalue_tok)


def copy_to(src, dst, send_sem, recv_sem, seq, span):
    return pltpu.make_async_remote_copy(
        src_ref=src,
        dst_ref=dst,
        send_sem=send_sem,
        recv_sem=recv_sem,
        device_id={"seq": seq, "span": span},
        device_id_type=pl.DeviceIdType.MESH,
    )


def fused_kernel(
    q_hbm, g_hbm, k_hbm, v_hbm, count_hbm, slot_hbm, weight_hbm,
    dq_ref, dk_ref, dv_ref,
    count_ref, slot_ref, weight_ref, k_ref, v_ref, kvin, rows, kv, q_all, g_all, picks_ref, mine_ref, dq_out,
    acc, pair_send, pair_got, cross_send, cross_got, back_send, back, pool_send, pool_got, stack_ref,
    in_sem, a_send, a_recv, z_send, z_recv, q_send, q_recv, g_send, g_recv, d_send, d_recv,
    pair_sems, cross_sems, b_send, b_recv, p_send, p_recv,
):
    n = 16
    lines = 4
    parts = kv.shape[0]
    wide = HEAD_DIM
    two = 2 * wide
    quarter = q_all.shape[2]
    chunks = tuple((2 * part, 2 * part + 2) for part in range(parts - 1))
    chunks = chunks + ((2 * parts - 2, 2 * parts - 1), (2 * parts - 1, 2 * parts))
    me = lax.axis_index("seq")
    span = lax.axis_index("span")
    other = 1 - span
    capacity = k_ref.shape[0]
    z, y, x = me // 4, (me // 2) % 2, me % 2
    own_line = me % 4
    x_line = own_line + 1 - 2 * x
    y_line = own_line + 2 - 4 * y
    d_line = 3 - own_line
    plane = (x_line, y_line, d_line)
    parity = z % 2
    half = z // 2
    in_half = me % 8
    middle = (z == 1) | (z == 2)
    z_pair = z + 1 - 2 * parity
    z_middle = 2 - half
    z_far = 3 - 3 * half
    z_near = 2 - half
    z_cross = (z + 2) % 4
    scale = HEAD_DIM ** (-0.5)
    to_exp2 = scale * math.log2(math.e)
    last = (((1,), (1,)), ((), ()))
    first = (((0,), (0,)), ((), ()))

    loads = [
        pltpu.make_async_copy(k_hbm, k_ref, in_sem.at[0]),
        pltpu.make_async_copy(v_hbm, v_ref, in_sem.at[1]),
    ]
    own_quarter = pl.ds(pl.multiple_of(own_line * quarter, 128), quarter)
    own_loads = [
        pltpu.make_async_copy(q_hbm.at[:, own_quarter], q_all.at[own_line], in_sem.at[2]),
        pltpu.make_async_copy(g_hbm.at[:, own_quarter], g_all.at[own_line], in_sem.at[3]),
    ]
    small_loads = [
        pltpu.make_async_copy(count_hbm, count_ref, in_sem.at[4]),
        pltpu.make_async_copy(slot_hbm, slot_ref, in_sem.at[5]),
        pltpu.make_async_copy(weight_hbm, weight_ref, in_sem.at[6]),
    ]
    for load in loads + small_loads + own_loads:
        load.start()
    barrier = pltpu.get_barrier_semaphore()
    for off in range(1, n):
        pl.semaphore_signal(
            barrier, inc=1, device_id={"seq": (me + off) % n, "span": span},
            device_id_type=pl.DeviceIdType.MESH,
        )
    for off in range(n // 2):
        pl.semaphore_signal(
            barrier, inc=1, device_id={"seq": half * 8 + (in_half + off) % 8, "span": other},
            device_id_type=pl.DeviceIdType.MESH,
        )
    for load in loads + small_loads:
        load.wait()
    for p in range(n):
        source = k_ref if p < n // 2 else v_ref
        for part in range(parts):
            start = ((p % lines) * 2 * parts + 2 * part + (p // lines) % 2) * wide
            kvin[part, p] = source[:, start : start + wide]
    pl.semaphore_wait(barrier, n - 1 + n // 2)

    def spread(part, off):
        p = (me + off) % n
        return copy_to(kvin.at[part, p], rows.at[part, me], a_send.at[part, off], a_recv.at[part, me], p, span)

    def spread_in(part, off):
        p = (me + off) % n
        return copy_to(kvin.at[part, p], rows.at[part, p], a_send.at[part, off], a_recv.at[part, p], p, span)

    offsets = (15, 1, 14, 2, 13, 3, 12, 4, 11, 5, 10, 6, 9, 7, 8)

    def send_memory(part):
        for off in offsets:
            spread(part, off).start()
        rows[part, me] = kvin[part, me]

    def exchange(part, t, whole, held, send_sem, recv_sem):
        line = plane[t]
        src = pl.ds(pl.multiple_of(line * quarter + part * two, 128), two)
        dst = pl.ds(part * two, two)
        return copy_to(
            whole.at[:, src], held.at[own_line, :, dst], send_sem.at[part, t], recv_sem.at[part, own_line],
            z * 4 + line, span,
        )

    def exchange_in(part, t, whole, held, send_sem, recv_sem):
        line = plane[t]
        dst = pl.ds(part * two, two)
        return copy_to(
            whole.at[:, dst], held.at[line, :, dst], send_sem.at[part, t], recv_sem.at[part, line],
            z * 4 + line, span,
        )

    queries = (q_hbm, q_all, q_send, q_recv)
    grads = (g_hbm, g_all, g_send, g_recv)
    def send_tokens(part):
        for t in range(3):
            exchange(part, t, *queries).start()
            exchange(part, t, *grads).start()

    @pl.when(span == 1)
    def _():
        send_memory(0)
        send_tokens(0)
        send_memory(1)

    @pl.when(span == 0)
    def _():
        send_tokens(0)
        send_memory(0)
        send_tokens(1)
        send_memory(1)


    def pool_move():
        return copy_to(pool_send, pool_got, p_send, p_recv, me, other)

    @pl.when(span == 1)
    def _():
        spots = lax.broadcasted_iota(jnp.int32, pool_send.shape, 0)
        total = jnp.zeros(pool_send.shape, F32)
        for j in range(slot_ref.shape[0]):
            total = total + jnp.where(spots == slot_ref[j : j + 1, :], weight_ref[j : j + 1, :], 0.0)
        pool_send[...] = total
        pool_move().start()

    slots = n * capacity
    counts = jnp.broadcast_to(count_ref[...], (8, n)).astype(F32).astype(BF)
    owner = lax.broadcasted_iota(jnp.int32, (n, slots), 1)
    below = lax.broadcasted_iota(jnp.int32, (n, slots), 0) * capacity
    ahead = jnp.where(owner >= below + capacity, 1.0, 0.0).astype(BF)
    inside = jnp.where((owner >= below) & (owner < below + capacity), 1.0, 0.0).astype(BF)
    position = jnp.where((owner >= below) & (owner < below + capacity), owner - below, 0)
    position = jnp.sum(position.astype(F32), axis=0, keepdims=True)
    offset = jnp.dot(counts, ahead, preferred_element_type=F32)[:1]
    length = jnp.dot(counts, inside, preferred_element_type=F32)[:1]
    place = jnp.where(position < length, offset + position, -1.0).astype(jnp.int32)
    picks = lax.broadcasted_iota(jnp.int32, (LIVE, slots), 0) == place
    picks_ref[...] = jnp.where(picks, 1.0, 0.0).astype(BF)

    @pl.when(span == 1)
    def _():
        mine = picks_ref[:, pl.ds(pl.multiple_of(half * (slots // 2), 128), slots // 2)]
        unit = lax.broadcasted_iota(jnp.int32, (LIVE, LIVE), 0) == lax.broadcasted_iota(jnp.int32, (LIVE, LIVE), 1)
        unit = jnp.where(unit, 1.0, 0.0).astype(BF)
        mine_ref[...] = lax.dot_general(mine, unit, first, preferred_element_type=F32).astype(BF)


    def along(part, source, target, k):
        block = kv.at[part, source]
        return copy_to(block, block, z_send.at[part, k], z_recv.at[part, source], target * 4 + own_line, span)

    def pack(part):
        for off in offsets:
            spread_in(part, off).wait_recv()
        packed = jnp.dot(picks_ref[...], rows[part].reshape(slots, wide), preferred_element_type=F32)
        kv[part, z] = packed.astype(BF)
        along(part, z, z_middle, 0).start()
        along(part, z, z_pair, 1).start()

    def relay(part):
        @pl.when(middle)
        def _():
            along(part, z_near, z_pair, 2).wait_recv()
            along(part, z_near, z_pair, 2).start()
            along(part, z_far, z_pair, 3).wait_recv()
            along(part, z_far, z_pair, 3).start()

    def gathered(part):
        along(part, z_pair, z_pair, 1).wait_recv()

        @pl.when(jnp.logical_not(middle))
        def _():
            along(part, z_near, z_pair, 2).wait_recv()
            along(part, z_far, z_pair, 3).wait_recv()

        for t in range(3):
            exchange_in(part, t, *queries).wait_recv()
            exchange_in(part, t, *grads).wait_recv()

    def dq_move(part, t):
        line = plane[t]
        src = pl.ds(part * two, two)
        dst = pl.ds(pl.multiple_of(own_line * quarter + part * two, 128), two)
        return copy_to(
            dq_out.at[line, :, src], dq_ref.at[:, dst], d_send.at[part, t], d_recv.at[part, own_line],
            z * 4 + line, span,
        )

    def dq_in(part, t):
        line = plane[t]
        src = pl.ds(part * two, two)
        dst = pl.ds(pl.multiple_of(line * quarter + part * two, 128), two)
        return copy_to(
            dq_out.at[line, :, src], dq_ref.at[:, dst], d_send.at[part, t], d_recv.at[part, line],
            z * 4 + line, span,
        )

    def one_head(part, b, with_memory):
        tokens = dq_out.shape[0] * dq_out.shape[1]
        here = slice((2 * part + b) * wide, (2 * part + b + 1) * wide)
        query = q_all[:, :, here].reshape(tokens, wide)
        grad = g_all[:, :, here].reshape(tokens, wide)
        key = kv[part, b]
        value = kv[part, 2 + b]
        scores = lax.dot_general(key, query, last, preferred_element_type=F32)
        shifted = jnp.exp2((scores - jnp.max(scores, axis=0, keepdims=True)) * to_exp2)
        probs = shifted * (1.0 / jnp.sum(shifted, axis=0, keepdims=True))
        low = probs.astype(BF)
        probs_grad = lax.dot_general(value, grad, last, preferred_element_type=F32)
        delta = jnp.sum(low.astype(F32) * probs_grad, axis=0, keepdims=True)
        scores_grad = (probs * (probs_grad - delta)).astype(BF)
        dq = lax.dot_general(scores_grad, key, first, preferred_element_type=F32) * scale
        dq_out[:, :, here] = dq.astype(BF).reshape(lines, tokens // lines, wide)
        if with_memory:
            acc[0, 2 * part + b] = jnp.dot(scores_grad, query, preferred_element_type=F32) * scale
            acc[1, 2 * part + b] = jnp.dot(low, grad, preferred_element_type=F32)

    def pair_move(chunk):
        heads = slice(*chunks[chunk])
        return copy_to(
            pair_send.at[heads], pair_got.at[heads], pair_sems.at[chunk, 0], pair_sems.at[chunk, 1],
            z_pair * 4 + own_line, span,
        )

    def compute(part):
        @pl.when(span == 1)
        def _():
            for b in range(2):
                one_head(part, b, True)
                for chunk, (lo, hi) in enumerate(chunks):
                    if hi == 2 * part + b + 1:
                        pair_send[lo:hi] = acc[1 - parity, lo:hi].astype(BF)
                        pair_move(chunk).start()

        @pl.when(span == 0)
        def _():
            for b in range(2):
                one_head(part, b, False)

    def send_dq(part):
        for t in range(3):
            dq_move(part, t).start()
        here = pl.ds(part * two, two)
        dst = pl.ds(pl.multiple_of(own_line * quarter + part * two, 128), two)
        dq_ref[:, dst] = dq_out[own_line, :, here]

    def cross_move(chunk):
        heads = slice(*chunks[chunk])
        return copy_to(
            cross_send.at[heads], cross_got.at[heads], cross_sems.at[chunk, 0], cross_sems.at[chunk, 1],
            z_cross * 4 + own_line, span,
        )

    def cross(chunk):
        lo, hi = chunks[chunk]

        @pl.when(span == 1)
        def _():
            pair_move(chunk).wait_recv()
            total = acc[parity, lo:hi] + pair_got[lo:hi].astype(F32)
            acc[parity, lo:hi] = total
            cross_send[lo:hi] = total.astype(BF)
            cross_move(chunk).start()

    def give(chunk, off):
        p = (in_half + off) % 8
        lo, hi = chunks[chunk]
        heads = pl.ds(lo, hi - lo)
        return copy_to(
            back_send.at[p, heads], back.at[in_half, heads], b_send.at[chunk, off], b_recv.at[chunk, in_half],
            half * 8 + p, other,
        )

    def hand_back(chunk):
        @pl.when(span == 1)
        def _():
            cross_move(chunk).wait_recv()
            for head in range(*chunks[chunk]):
                total = acc[parity, head] + cross_got[head].astype(F32)
                high = total.astype(BF)
                rest = (total - high.astype(F32)).astype(BF)
                both = jnp.concatenate([high, rest], axis=1)
                owned = jnp.dot(mine_ref[...], both, preferred_element_type=F32).astype(BF)
                back_send[:, head, 0] = owned[:, :wide].reshape(n // 2, capacity, wide)
                back_send[:, head, 1] = owned[:, wide:].reshape(n // 2, capacity, wide)
            for off in range(n // 2):
                give(chunk, off).start()

    @pl.when(span == 0)
    def _():
        pool_move().wait_recv()
        matrix = pool_got[...]
        high = matrix.astype(BF)
        stack_ref[: matrix.shape[0]] = high
        stack_ref[matrix.shape[0] :] = (matrix - high.astype(F32)).astype(BF)

    def pool(chunk):
        lo, hi = chunks[chunk]
        tokens_here = dq_out.shape[1]

        @pl.when(span == 0)
        def _():
            stacked = stack_ref[...]
            high = stacked[:tokens_here]
            heads = pl.ds(lo, hi - lo)
            for p in range(n // 2):
                copy_to(
                    back_send.at[p, heads], back.at[p, heads], b_send.at[chunk, p], b_recv.at[chunk, p], me, other
                ).wait_recv()
            for head in range(lo, hi):
                for kind, result in enumerate((dk_ref, dv_ref)):
                    upper = jnp.concatenate([back[kind * lines + i, head, 0] for i in range(lines)], axis=1)
                    lower = jnp.concatenate([back[kind * lines + i, head, 1] for i in range(lines)], axis=1)
                    tokens = jnp.dot(stacked, upper, preferred_element_type=F32)
                    tokens = tokens[: tokens_here] + tokens[tokens_here :]
                    tokens = tokens + jnp.dot(high, lower, preferred_element_type=F32)
                    tokens = tokens.astype(BF)
                    for i in range(lines):
                        start = (i * 2 * parts + head) * wide
                        result[:, start : start + wide] = tokens[:, i * wide : (i + 1) * wide]

    @pl.when(span == 1)
    def _():
        pack(0)
        send_memory(2)
        send_tokens(1)
        pack(1)
        relay(0)
        send_tokens(2)
        pack(2)
        relay(1)

    @pl.when(span == 0)
    def _():
        pack(0)
        send_memory(2)
        pack(1)
        relay(0)
        send_tokens(2)
        pack(2)
        relay(1)

    for load in own_loads:
        load.wait()
    gathered(0)
    compute(0)
    send_dq(0)
    relay(2)
    gathered(1)
    compute(1)
    send_dq(1)
    cross(0)
    cross(1)
    gathered(2)
    compute(2)
    send_dq(2)
    hand_back(0)
    cross(2)
    cross(3)
    hand_back(1)
    hand_back(2)
    hand_back(3)
    pool(0)
    pool(1)
    pool(2)
    pool(3)

    @pl.when(span == 1)
    def _():
        dk_ref[...] = jnp.zeros(dk_ref.shape, BF)
        dv_ref[...] = jnp.zeros(dv_ref.shape, BF)

    for part in range(parts):
        for t in range(3):
            dq_in(part, t).wait_recv()
    for part in range(parts):
        for off in offsets:
            spread(part, off).wait_send()
        for t in range(3):
            exchange(part, t, *queries).wait_send()
            exchange(part, t, *grads).wait_send()
            dq_move(part, t).wait_send()
        along(part, z, z_middle, 0).wait_send()
        along(part, z, z_pair, 1).wait_send()

    @pl.when(middle)
    def _():
        for part in range(parts):
            along(part, z_near, z_pair, 2).wait_send()
            along(part, z_far, z_pair, 3).wait_send()

    @pl.when(span == 1)
    def _():
        pool_move().wait_send()
        for chunk in range(len(chunks)):
            pair_move(chunk).wait_send()
            cross_move(chunk).wait_send()
            for off in range(n // 2):
                give(chunk, off).wait_send()


def settle_kernel(dq_in, dk_in, dv_in, dq_ref, dk_ref, dv_ref, sems):
    moves = [
        pltpu.make_async_copy(src, dst, sems.at[i])
        for i, (src, dst) in enumerate(((dq_in, dq_ref), (dk_in, dk_ref), (dv_in, dv_ref)))
    ]
    for move in moves:
        move.start()
    for move in moves:
        move.wait()


def per_device_fused(query, dout, mem_key, mem_value, keep_count, keep_slot, pool_weight):
    n = 16
    lines = 4
    tokens, width = query.shape[1:]
    capacity = mem_key.shape[1]
    quarter = width // lines
    parts = quarter // (2 * HEAD_DIM)
    vmem = pl.BlockSpec(memory_space=pltpu.VMEM)
    hbm = pl.BlockSpec(memory_space=pltpu.HBM)
    dma = pltpu.SemaphoreType.DMA
    out = jax.ShapeDtypeStruct((tokens, width), BF)
    heads = 2 * parts
    owned = (n // 2, heads, 2, capacity, HEAD_DIM)
    dq, dk, dv = pl.pallas_call(
        fused_kernel,
        out_shape=(out, out, out),
        in_specs=[hbm] * 7,
        out_specs=(vmem, vmem, vmem),
        scratch_shapes=[
            pltpu.VMEM(keep_count.shape, jnp.int32),
            pltpu.VMEM((keep_slot.shape[2], capacity), jnp.int32),
            pltpu.VMEM((keep_slot.shape[2], capacity), F32),
            pltpu.VMEM((capacity, width), BF),
            pltpu.VMEM((capacity, width), BF),
            pltpu.VMEM((parts, n, capacity, HEAD_DIM), BF),
            pltpu.VMEM((parts, n, capacity, HEAD_DIM), BF),
            pltpu.VMEM((parts, 4, LIVE, HEAD_DIM), BF),
            pltpu.VMEM((lines, tokens, quarter), BF),
            pltpu.VMEM((lines, tokens, quarter), BF),
            pltpu.VMEM((LIVE, n * capacity), BF),
            pltpu.VMEM((n // 2 * capacity, LIVE), BF),
            pltpu.VMEM((lines, tokens, quarter), BF),
            pltpu.VMEM((2, heads, LIVE, HEAD_DIM), F32),
            pltpu.VMEM((heads, LIVE, HEAD_DIM), BF),
            pltpu.VMEM((heads, LIVE, HEAD_DIM), BF),
            pltpu.VMEM((heads, LIVE, HEAD_DIM), BF),
            pltpu.VMEM((heads, LIVE, HEAD_DIM), BF),
            pltpu.VMEM(owned, BF),
            pltpu.VMEM(owned, BF),
            pltpu.VMEM((tokens, capacity), F32),
            pltpu.VMEM((tokens, capacity), F32),
            pltpu.VMEM((2 * tokens, capacity), BF),
            dma((7,)), dma((parts, n)), dma((parts, n)), dma((parts, 4)), dma((parts, 4)),
            dma((parts, 3)), dma((parts, lines)), dma((parts, 3)), dma((parts, lines)),
            dma((parts, 3)), dma((parts, lines)),
            dma((parts + 1, 2)), dma((parts + 1, 2)), dma((parts + 1, n // 2)), dma((parts + 1, n // 2)), dma, dma,
        ],
        compiler_params=pltpu.CompilerParams(
            collective_id=0, has_side_effects=True, vmem_limit_bytes=32 << 20
        ),
    )(
        *(
            pltpu.with_memory_space_constraint(value, pltpu.HBM)
            for value in (
                query[0], dout[0], mem_key[0], mem_value[0], keep_count, keep_slot[0].T, pool_weight[0].T,
            )
        )
    )
    any_space = pl.BlockSpec(memory_space=pl.ANY)
    dq, dk, dv = pl.pallas_call(
        settle_kernel,
        out_shape=(out, out, out),
        in_specs=[any_space] * 3,
        out_specs=(any_space,) * 3,
        scratch_shapes=[dma((3,))],
        compiler_params=pltpu.CompilerParams(vmem_limit_bytes=32 << 20),
    )(dq, dk, dv)
    return dq[None], dk[None], dv[None]


def solution(mesh):
    fused = mesh.shape["seq"] == 16 and mesh.shape["span"] == 2
    return jax.shard_map(
        per_device_fused if fused else per_device,
        mesh=mesh,
        in_specs=(
            P("span", "seq", None),
            P("span", "seq", None),
            P("span", "seq", None),
            P("span", "seq", None),
            P("span", None),
            P("span", "seq", None),
            P("span", "seq", None),
        ),
        out_specs=(P("span", "seq", None), P("span", "seq", None), P("span", "seq", None)),
        check_vma=False,
    )
```

```python
import math

import jax
import jax.numpy as jnp
from jax import lax
from jax.experimental import pallas as pl
from jax.experimental.pallas import tpu as pltpu
from jax.sharding import PartitionSpec as P

HEAD_DIM = 128
LIVE = 256
BF = jnp.bfloat16
F32 = jnp.float32


def passed_along(block, axis, distance):
    devices = range(lax.axis_size(axis))
    route = [(i - distance, i) for i in devices if i - distance in devices]
    return lax.ppermute(block, axis, route)


def head_backward(query_head, grad_head, key_head, value_head, live_mask, block_rows):
    score_scale = key_head.shape[1] ** (-0.5)
    head_width = query_head.shape[1]
    blocks = query_head.shape[0] // block_rows
    query_blocks = query_head.reshape(blocks, block_rows, head_width)
    grad_blocks = grad_head.reshape(blocks, block_rows, head_width)

    def visit_block(totals, inputs):
        key_grad, value_grad = totals
        query_block, grad_block = inputs
        scores = jnp.dot(query_block, key_head.T, preferred_element_type=jnp.float32) * score_scale
        scores = jnp.where(live_mask[None, :], scores, -jnp.inf)
        shifted = jnp.exp(scores - jnp.max(scores, axis=1, keepdims=True))
        probs_full = shifted / jnp.sum(shifted, axis=1, keepdims=True)
        probs_low = probs_full.astype(jnp.bfloat16)
        attn_out = jnp.dot(probs_low, value_head, preferred_element_type=jnp.float32)
        deltas = jnp.sum(grad_block.astype(jnp.float32) * attn_out, axis=1, keepdims=True)
        probs_grad = jnp.dot(grad_block, value_head.T, preferred_element_type=jnp.float32)
        scores_grad = (probs_full * (probs_grad - deltas)).astype(jnp.bfloat16)
        query_grad = (
            jnp.dot(scores_grad, key_head, preferred_element_type=jnp.float32) * score_scale
        ).astype(jnp.bfloat16)
        key_grad = (
            key_grad
            + lax.dot_general(
                scores_grad,
                query_block,
                (((0,), (0,)), ((), ())),
                preferred_element_type=jnp.float32,
            )
            * score_scale
        )
        value_grad = value_grad + lax.dot_general(
            probs_low, grad_block, (((0,), (0,)), ((), ())), preferred_element_type=jnp.float32
        )
        return ((key_grad, value_grad), query_grad)

    empty_grad = jnp.zeros(key_head.shape, jnp.float32)
    (key_grad, value_grad), query_grad = lax.scan(
        visit_block, (empty_grad, empty_grad), (query_blocks, grad_blocks)
    )
    return (query_grad.reshape(-1, head_width), key_grad, value_grad)


def owner_rows(key_parts, value_parts, token_parts, groups, row_count):
    got_key, got_value = (
        lax.all_to_all(key_parts, "seq", split_axis=0, concat_axis=0, tiled=True),
        lax.all_to_all(value_parts, "seq", split_axis=0, concat_axis=0, tiled=True),
    )

    def fold_parts(values):
        shaped = values.reshape(token_parts, groups, row_count, values.shape[2], values.shape[3])
        summed = jnp.sum(shaped, axis=0)
        return summed.transpose(1, 0, 2, 3).reshape(row_count, -1)

    return (fold_parts(got_key), fold_parts(got_value))


def pool_matrix(slots, weights, local_tokens):
    positions = jnp.arange(local_tokens)
    onehot = (slots[:, :, None] == positions[None, None, :]).astype(jnp.float32)
    return jnp.einsum("cjt,cj->tc", onehot, weights, precision=lax.Precision.HIGHEST)


def apply_pool(matrix, key_rows, value_rows):
    stacked = jnp.concatenate([key_rows, value_rows], axis=1)
    return jnp.dot(
        matrix, stacked, precision=lax.Precision.HIGHEST, preferred_element_type=jnp.float32
    )


def per_device(query, dout, mem_key, mem_value, keep_count, keep_slot, pool_weight):
    devices = lax.axis_size("seq")
    head_width = HEAD_DIM
    head_count = query.shape[2] // head_width
    groups = math.gcd(head_count, devices)
    token_parts = devices // groups
    group_heads = head_count // groups
    local_tokens = query.shape[1]
    part_rows = local_tokens // token_parts
    capacity = mem_key.shape[1]
    owner_counts = keep_count[0]

    def token_layout(values):
        shaped = values.reshape(token_parts, part_rows, groups, group_heads, head_width)
        return shaped.transpose(0, 2, 1, 3, 4).reshape(devices, part_rows, group_heads, head_width)

    def memory_layout(values):
        row_count = values.shape[0]
        shaped = values.reshape(row_count, groups, group_heads, head_width).transpose(1, 0, 2, 3)
        spread = jnp.broadcast_to(shaped[None], (token_parts,) + shaped.shape)
        return spread.reshape(devices, row_count, group_heads, head_width)

    slot_index = jnp.arange(devices * capacity)
    live_mask = slot_index % capacity < jnp.repeat(owner_counts, capacity)
    key_used, value_used = (mem_key[0], mem_value[0])
    query_rows = lax.all_to_all(
        token_layout(query[0]), "seq", split_axis=0, concat_axis=0, tiled=True
    )
    grad_rows = lax.all_to_all(
        token_layout(dout[0]), "seq", split_axis=0, concat_axis=0, tiled=True
    )
    key_rows = lax.all_to_all(
        memory_layout(key_used), "seq", split_axis=0, concat_axis=0, tiled=True
    )
    value_rows = lax.all_to_all(
        memory_layout(value_used), "seq", split_axis=0, concat_axis=0, tiled=True
    )
    item_heads = query_rows.shape[2]
    row_count = key_rows.shape[1]
    query_total = devices * part_rows
    block_rows = 512
    query_flat = jnp.moveaxis(query_rows.reshape(query_total, item_heads, head_width), 1, 0)
    grad_flat = jnp.moveaxis(grad_rows.reshape(query_total, item_heads, head_width), 1, 0)
    key_flat = jnp.moveaxis(key_rows.reshape(devices * row_count, item_heads, head_width), 1, 0)
    value_flat = jnp.moveaxis(value_rows.reshape(devices * row_count, item_heads, head_width), 1, 0)

    def one_head(pieces):
        return head_backward(pieces[0], pieces[1], pieces[2], pieces[3], live_mask, block_rows)

    query_grad, key_grad, value_grad = lax.map(
        one_head, (query_flat, grad_flat, key_flat, value_flat)
    )
    query_back = jnp.moveaxis(query_grad, 0, 1).reshape(devices, part_rows, item_heads, head_width)
    key_back = jnp.moveaxis(key_grad, 0, 1).reshape(devices, row_count, item_heads, head_width)
    value_back = jnp.moveaxis(value_grad, 0, 1).reshape(devices, row_count, item_heads, head_width)
    returned = lax.all_to_all(query_back, "seq", split_axis=0, concat_axis=0, tiled=True)
    returned = returned.reshape(token_parts, groups, part_rows, group_heads, head_width).transpose(
        0, 2, 1, 3, 4
    )
    dquery = returned.reshape(1, local_tokens, groups * group_heads * head_width)
    matrix = pool_matrix(keep_slot[0], pool_weight[0], local_tokens)
    key_rows, value_rows = owner_rows(key_back, value_back, token_parts, groups, capacity)
    local_grad = apply_pool(matrix, key_rows, value_rows).astype(jnp.bfloat16)
    tokens_grad = passed_along(local_grad, "span", -1)
    feature_width = groups * group_heads * head_width
    dkey_tok = tokens_grad[None, :, :feature_width]
    dvalue_tok = tokens_grad[None, :, feature_width:]
    return (dquery, dkey_tok, dvalue_tok)


def copy_to(src, dst, send_sem, recv_sem, seq, span):
    return pltpu.make_async_remote_copy(
        src_ref=src,
        dst_ref=dst,
        send_sem=send_sem,
        recv_sem=recv_sem,
        device_id={"seq": seq, "span": span},
        device_id_type=pl.DeviceIdType.MESH,
    )


def fused_kernel(
    q_hbm, g_hbm, k_hbm, v_hbm, count_hbm, slot_hbm, weight_hbm,
    dq_ref, dk_ref, dv_ref,
    count_ref, slot_ref, weight_ref, k_ref, v_ref, kvin, rows, kv, q_all, g_all, picks_ref, mine_ref, dq_out,
    acc, pair_send, pair_got, cross_send, cross_got, back_send, back, pool_send, pool_got, stack_ref,
    in_sem, a_send, a_recv, z_send, z_recv, q_send, q_recv, g_send, g_recv, d_send, d_recv,
    pair_sems, cross_sems, b_send, b_recv, p_send, p_recv,
):
    n = 16
    lines = 4
    parts = kv.shape[0]
    wide = HEAD_DIM
    two = 2 * wide
    quarter = q_all.shape[2]
    chunks = tuple((2 * part, 2 * part + 2) for part in range(parts - 1))
    chunks = chunks + ((2 * parts - 2, 2 * parts - 1), (2 * parts - 1, 2 * parts))
    me = lax.axis_index("seq")
    span = lax.axis_index("span")
    other = 1 - span
    capacity = k_ref.shape[0]
    z, y, x = me // 4, (me // 2) % 2, me % 2
    own_line = me % 4
    x_line = own_line + 1 - 2 * x
    y_line = own_line + 2 - 4 * y
    d_line = 3 - own_line
    plane = (x_line, y_line, d_line)
    parity = z % 2
    half = z // 2
    in_half = me % 8
    middle = (z == 1) | (z == 2)
    z_pair = z + 1 - 2 * parity
    z_middle = 2 - half
    z_far = 3 - 3 * half
    z_near = 2 - half
    z_cross = (z + 2) % 4
    scale = HEAD_DIM ** (-0.5)
    to_exp2 = scale * math.log2(math.e)
    last = (((1,), (1,)), ((), ()))
    first = (((0,), (0,)), ((), ()))

    loads = [
        pltpu.make_async_copy(k_hbm, k_ref, in_sem.at[0]),
        pltpu.make_async_copy(v_hbm, v_ref, in_sem.at[1]),
    ]
    own_quarter = pl.ds(pl.multiple_of(own_line * quarter, 128), quarter)
    own_loads = [
        pltpu.make_async_copy(q_hbm.at[:, own_quarter], q_all.at[own_line], in_sem.at[2]),
        pltpu.make_async_copy(g_hbm.at[:, own_quarter], g_all.at[own_line], in_sem.at[3]),
    ]
    small_loads = [
        pltpu.make_async_copy(count_hbm, count_ref, in_sem.at[4]),
        pltpu.make_async_copy(slot_hbm, slot_ref, in_sem.at[5]),
        pltpu.make_async_copy(weight_hbm, weight_ref, in_sem.at[6]),
    ]
    for load in loads + small_loads + own_loads:
        load.start()
    barrier = pltpu.get_barrier_semaphore()
    for off in range(1, n):
        pl.semaphore_signal(
            barrier, inc=1, device_id={"seq": (me + off) % n, "span": span},
            device_id_type=pl.DeviceIdType.MESH,
        )
    for off in range(n // 2):
        pl.semaphore_signal(
            barrier, inc=1, device_id={"seq": half * 8 + (in_half + off) % 8, "span": other},
            device_id_type=pl.DeviceIdType.MESH,
        )
    for load in loads + small_loads:
        load.wait()
    for p in range(n):
        source = k_ref if p < n // 2 else v_ref
        for part in range(parts):
            start = ((p % lines) * 2 * parts + 2 * part + (p // lines) % 2) * wide
            kvin[part, p] = source[:, start : start + wide]
    pl.semaphore_wait(barrier, n - 1 + n // 2)

    def spread(part, off):
        p = (me + off) % n
        return copy_to(kvin.at[part, p], rows.at[part, me], a_send.at[part, off], a_recv.at[part, me], p, span)

    def spread_in(part, off):
        p = (me + off) % n
        return copy_to(kvin.at[part, p], rows.at[part, p], a_send.at[part, off], a_recv.at[part, p], p, span)

    offsets = (15, 1, 14, 2, 13, 3, 12, 4, 11, 5, 10, 6, 9, 7, 8)

    def send_memory(part):
        for off in offsets:
            spread(part, off).start()
        rows[part, me] = kvin[part, me]

    def exchange(part, t, whole, held, send_sem, recv_sem):
        line = plane[t]
        src = pl.ds(pl.multiple_of(line * quarter + part * two, 128), two)
        dst = pl.ds(part * two, two)
        return copy_to(
            whole.at[:, src], held.at[own_line, :, dst], send_sem.at[part, t], recv_sem.at[part, own_line],
            z * 4 + line, span,
        )

    def exchange_in(part, t, whole, held, send_sem, recv_sem):
        line = plane[t]
        dst = pl.ds(part * two, two)
        return copy_to(
            whole.at[:, dst], held.at[line, :, dst], send_sem.at[part, t], recv_sem.at[part, line],
            z * 4 + line, span,
        )

    queries = (q_hbm, q_all, q_send, q_recv)
    grads = (g_hbm, g_all, g_send, g_recv)
    def send_tokens(part):
        for t in range(3):
            exchange(part, t, *queries).start()
            exchange(part, t, *grads).start()

    @pl.when(span == 1)
    def _():
        send_memory(0)
        send_tokens(0)
        send_memory(1)

    @pl.when(span == 0)
    def _():
        send_tokens(0)
        send_memory(0)
        send_tokens(1)
        send_memory(1)


    def pool_move():
        return copy_to(pool_send, pool_got, p_send, p_recv, me, other)

    @pl.when(span == 1)
    def _():
        spots = lax.broadcasted_iota(jnp.int32, pool_send.shape, 0)
        total = jnp.zeros(pool_send.shape, F32)
        for j in range(slot_ref.shape[0]):
            total = total + jnp.where(spots == slot_ref[j : j + 1, :], weight_ref[j : j + 1, :], 0.0)
        pool_send[...] = total
        pool_move().start()

    slots = n * capacity
    counts = jnp.broadcast_to(count_ref[...], (8, n)).astype(F32).astype(BF)
    owner = lax.broadcasted_iota(jnp.int32, (n, slots), 1)
    below = lax.broadcasted_iota(jnp.int32, (n, slots), 0) * capacity
    ahead = jnp.where(owner >= below + capacity, 1.0, 0.0).astype(BF)
    inside = jnp.where((owner >= below) & (owner < below + capacity), 1.0, 0.0).astype(BF)
    position = jnp.where((owner >= below) & (owner < below + capacity), owner - below, 0)
    position = jnp.sum(position.astype(F32), axis=0, keepdims=True)
    offset = jnp.dot(counts, ahead, preferred_element_type=F32)[:1]
    length = jnp.dot(counts, inside, preferred_element_type=F32)[:1]
    place = jnp.where(position < length, offset + position, -1.0).astype(jnp.int32)
    picks = lax.broadcasted_iota(jnp.int32, (LIVE, slots), 0) == place
    picks_ref[...] = jnp.where(picks, 1.0, 0.0).astype(BF)

    @pl.when(span == 1)
    def _():
        mine = picks_ref[:, pl.ds(pl.multiple_of(half * (slots // 2), 128), slots // 2)]
        unit = lax.broadcasted_iota(jnp.int32, (LIVE, LIVE), 0) == lax.broadcasted_iota(jnp.int32, (LIVE, LIVE), 1)
        unit = jnp.where(unit, 1.0, 0.0).astype(BF)
        mine_ref[...] = lax.dot_general(mine, unit, first, preferred_element_type=F32).astype(BF)


    def along(part, source, target, k):
        block = kv.at[part, source]
        return copy_to(block, block, z_send.at[part, k], z_recv.at[part, source], target * 4 + own_line, span)

    def pack(part):
        for off in offsets:
            spread_in(part, off).wait_recv()
        packed = jnp.dot(picks_ref[...], rows[part].reshape(slots, wide), preferred_element_type=F32)
        kv[part, z] = packed.astype(BF)
        along(part, z, z_middle, 0).start()
        along(part, z, z_pair, 1).start()

    def relay(part):
        @pl.when(middle)
        def _():
            along(part, z_near, z_pair, 2).wait_recv()
            along(part, z_near, z_pair, 2).start()
            along(part, z_far, z_pair, 3).wait_recv()
            along(part, z_far, z_pair, 3).start()

    def gathered(part):
        along(part, z_pair, z_pair, 1).wait_recv()

        @pl.when(jnp.logical_not(middle))
        def _():
            along(part, z_near, z_pair, 2).wait_recv()
            along(part, z_far, z_pair, 3).wait_recv()

        for t in range(3):
            exchange_in(part, t, *queries).wait_recv()
            exchange_in(part, t, *grads).wait_recv()

    def dq_move(part, t):
        line = plane[t]
        src = pl.ds(part * two, two)
        dst = pl.ds(pl.multiple_of(own_line * quarter + part * two, 128), two)
        return copy_to(
            dq_out.at[line, :, src], dq_ref.at[:, dst], d_send.at[part, t], d_recv.at[part, own_line],
            z * 4 + line, span,
        )

    def dq_in(part, t):
        line = plane[t]
        src = pl.ds(part * two, two)
        dst = pl.ds(pl.multiple_of(line * quarter + part * two, 128), two)
        return copy_to(
            dq_out.at[line, :, src], dq_ref.at[:, dst], d_send.at[part, t], d_recv.at[part, line],
            z * 4 + line, span,
        )

    def one_head(part, b, with_memory):
        tokens = dq_out.shape[0] * dq_out.shape[1]
        here = slice((2 * part + b) * wide, (2 * part + b + 1) * wide)
        query = q_all[:, :, here].reshape(tokens, wide)
        grad = g_all[:, :, here].reshape(tokens, wide)
        key = kv[part, b]
        value = kv[part, 2 + b]
        scores = lax.dot_general(key, query, last, preferred_element_type=F32)
        shifted = jnp.exp2((scores - jnp.max(scores, axis=0, keepdims=True)) * to_exp2)
        probs = shifted * (1.0 / jnp.sum(shifted, axis=0, keepdims=True))
        low = probs.astype(BF)
        probs_grad = lax.dot_general(value, grad, last, preferred_element_type=F32)
        delta = jnp.sum(low.astype(F32) * probs_grad, axis=0, keepdims=True)
        scores_grad = (probs * (probs_grad - delta)).astype(BF)
        dq = lax.dot_general(scores_grad, key, first, preferred_element_type=F32) * scale
        dq_out[:, :, here] = dq.astype(BF).reshape(lines, tokens // lines, wide)
        if with_memory:
            acc[0, 2 * part + b] = jnp.dot(scores_grad, query, preferred_element_type=F32) * scale
            acc[1, 2 * part + b] = jnp.dot(low, grad, preferred_element_type=F32)

    def pair_move(chunk):
        heads = slice(*chunks[chunk])
        return copy_to(
            pair_send.at[heads], pair_got.at[heads], pair_sems.at[chunk, 0], pair_sems.at[chunk, 1],
            z_pair * 4 + own_line, span,
        )

    def compute(part):
        @pl.when(span == 1)
        def _():
            for b in range(2):
                one_head(part, b, True)
                for chunk, (lo, hi) in enumerate(chunks):
                    if hi == 2 * part + b + 1:
                        pair_send[lo:hi] = acc[1 - parity, lo:hi].astype(BF)
                        pair_move(chunk).start()

        @pl.when(span == 0)
        def _():
            for b in range(2):
                one_head(part, b, False)

    def send_dq(part):
        for t in range(3):
            dq_move(part, t).start()
        here = pl.ds(part * two, two)
        dst = pl.ds(pl.multiple_of(own_line * quarter + part * two, 128), two)
        dq_ref[:, dst] = dq_out[own_line, :, here]

    def cross_move(chunk):
        heads = slice(*chunks[chunk])
        return copy_to(
            cross_send.at[heads], cross_got.at[heads], cross_sems.at[chunk, 0], cross_sems.at[chunk, 1],
            z_cross * 4 + own_line, span,
        )

    def cross(chunk):
        lo, hi = chunks[chunk]

        @pl.when(span == 1)
        def _():
            pair_move(chunk).wait_recv()
            total = acc[parity, lo:hi] + pair_got[lo:hi].astype(F32)
            acc[parity, lo:hi] = total
            cross_send[lo:hi] = total.astype(BF)
            cross_move(chunk).start()

    def give(chunk, off):
        p = (in_half + off) % 8
        lo, hi = chunks[chunk]
        heads = pl.ds(lo, hi - lo)
        return copy_to(
            back_send.at[p, heads], back.at[in_half, heads], b_send.at[chunk, off], b_recv.at[chunk, in_half],
            half * 8 + p, other,
        )

    def hand_back(chunk):
        @pl.when(span == 1)
        def _():
            cross_move(chunk).wait_recv()
            for head in range(*chunks[chunk]):
                total = acc[parity, head] + cross_got[head].astype(F32)
                high = total.astype(BF)
                rest = (total - high.astype(F32)).astype(BF)
                both = jnp.concatenate([high, rest], axis=1)
                owned = jnp.dot(mine_ref[...], both, preferred_element_type=F32).astype(BF)
                back_send[:, head, 0] = owned[:, :wide].reshape(n // 2, capacity, wide)
                back_send[:, head, 1] = owned[:, wide:].reshape(n // 2, capacity, wide)
            for off in range(n // 2):
                give(chunk, off).start()

    @pl.when(span == 0)
    def _():
        pool_move().wait_recv()
        matrix = pool_got[...]
        high = matrix.astype(BF)
        stack_ref[: matrix.shape[0]] = high
        stack_ref[matrix.shape[0] :] = (matrix - high.astype(F32)).astype(BF)

    def pool(chunk):
        lo, hi = chunks[chunk]
        tokens_here = dq_out.shape[1]

        @pl.when(span == 0)
        def _():
            stacked = stack_ref[...]
            high = stacked[:tokens_here]
            heads = pl.ds(lo, hi - lo)
            for p in range(n // 2):
                copy_to(
                    back_send.at[p, heads], back.at[p, heads], b_send.at[chunk, p], b_recv.at[chunk, p], me, other
                ).wait_recv()
            for head in range(lo, hi):
                for kind, result in enumerate((dk_ref, dv_ref)):
                    upper = jnp.concatenate([back[kind * lines + i, head, 0] for i in range(lines)], axis=1)
                    lower = jnp.concatenate([back[kind * lines + i, head, 1] for i in range(lines)], axis=1)
                    tokens = jnp.dot(stacked, upper, preferred_element_type=F32)
                    tokens = tokens[: tokens_here] + tokens[tokens_here :]
                    tokens = tokens + jnp.dot(high, lower, preferred_element_type=F32)
                    tokens = tokens.astype(BF)
                    for i in range(lines):
                        start = (i * 2 * parts + head) * wide
                        result[:, start : start + wide] = tokens[:, i * wide : (i + 1) * wide]

    @pl.when(span == 1)
    def _():
        pack(0)
        send_memory(2)
        send_tokens(1)
        pack(1)
        relay(0)
        send_tokens(2)
        pack(2)
        relay(1)

    @pl.when(span == 0)
    def _():
        pack(0)
        send_memory(2)
        send_tokens(2)
        pack(1)
        relay(0)
        pack(2)
        relay(1)

    for load in own_loads:
        load.wait()
    gathered(0)
    compute(0)
    send_dq(0)
    relay(2)
    gathered(1)
    compute(1)
    send_dq(1)
    cross(0)
    cross(1)
    gathered(2)
    compute(2)
    send_dq(2)
    hand_back(0)
    cross(2)
    cross(3)
    hand_back(1)
    hand_back(2)
    hand_back(3)
    pool(0)
    pool(1)
    pool(2)
    pool(3)

    @pl.when(span == 1)
    def _():
        dk_ref[...] = jnp.zeros(dk_ref.shape, BF)
        dv_ref[...] = jnp.zeros(dv_ref.shape, BF)

    for part in range(parts):
        for t in range(3):
            dq_in(part, t).wait_recv()
    for part in range(parts):
        for off in offsets:
            spread(part, off).wait_send()
        for t in range(3):
            exchange(part, t, *queries).wait_send()
            exchange(part, t, *grads).wait_send()
            dq_move(part, t).wait_send()
        along(part, z, z_middle, 0).wait_send()
        along(part, z, z_pair, 1).wait_send()

    @pl.when(middle)
    def _():
        for part in range(parts):
            along(part, z_near, z_pair, 2).wait_send()
            along(part, z_far, z_pair, 3).wait_send()

    @pl.when(span == 1)
    def _():
        pool_move().wait_send()
        for chunk in range(len(chunks)):
            pair_move(chunk).wait_send()
            cross_move(chunk).wait_send()
            for off in range(n // 2):
                give(chunk, off).wait_send()


def settle_kernel(dq_in, dk_in, dv_in, dq_ref, dk_ref, dv_ref, sems):
    moves = [
        pltpu.make_async_copy(src, dst, sems.at[i])
        for i, (src, dst) in enumerate(((dq_in, dq_ref), (dk_in, dk_ref), (dv_in, dv_ref)))
    ]
    for move in moves:
        move.start()
    for move in moves:
        move.wait()


def per_device_fused(query, dout, mem_key, mem_value, keep_count, keep_slot, pool_weight):
    n = 16
    lines = 4
    tokens, width = query.shape[1:]
    capacity = mem_key.shape[1]
    quarter = width // lines
    parts = quarter // (2 * HEAD_DIM)
    vmem = pl.BlockSpec(memory_space=pltpu.VMEM)
    hbm = pl.BlockSpec(memory_space=pltpu.HBM)
    dma = pltpu.SemaphoreType.DMA
    out = jax.ShapeDtypeStruct((tokens, width), BF)
    heads = 2 * parts
    owned = (n // 2, heads, 2, capacity, HEAD_DIM)
    dq, dk, dv = pl.pallas_call(
        fused_kernel,
        out_shape=(out, out, out),
        in_specs=[hbm] * 7,
        out_specs=(vmem, vmem, vmem),
        scratch_shapes=[
            pltpu.VMEM(keep_count.shape, jnp.int32),
            pltpu.VMEM((keep_slot.shape[2], capacity), jnp.int32),
            pltpu.VMEM((keep_slot.shape[2], capacity), F32),
            pltpu.VMEM((capacity, width), BF),
            pltpu.VMEM((capacity, width), BF),
            pltpu.VMEM((parts, n, capacity, HEAD_DIM), BF),
            pltpu.VMEM((parts, n, capacity, HEAD_DIM), BF),
            pltpu.VMEM((parts, 4, LIVE, HEAD_DIM), BF),
            pltpu.VMEM((lines, tokens, quarter), BF),
            pltpu.VMEM((lines, tokens, quarter), BF),
            pltpu.VMEM((LIVE, n * capacity), BF),
            pltpu.VMEM((n // 2 * capacity, LIVE), BF),
            pltpu.VMEM((lines, tokens, quarter), BF),
            pltpu.VMEM((2, heads, LIVE, HEAD_DIM), F32),
            pltpu.VMEM((heads, LIVE, HEAD_DIM), BF),
            pltpu.VMEM((heads, LIVE, HEAD_DIM), BF),
            pltpu.VMEM((heads, LIVE, HEAD_DIM), BF),
            pltpu.VMEM((heads, LIVE, HEAD_DIM), BF),
            pltpu.VMEM(owned, BF),
            pltpu.VMEM(owned, BF),
            pltpu.VMEM((tokens, capacity), F32),
            pltpu.VMEM((tokens, capacity), F32),
            pltpu.VMEM((2 * tokens, capacity), BF),
            dma((7,)), dma((parts, n)), dma((parts, n)), dma((parts, 4)), dma((parts, 4)),
            dma((parts, 3)), dma((parts, lines)), dma((parts, 3)), dma((parts, lines)),
            dma((parts, 3)), dma((parts, lines)),
            dma((parts + 1, 2)), dma((parts + 1, 2)), dma((parts + 1, n // 2)), dma((parts + 1, n // 2)), dma, dma,
        ],
        compiler_params=pltpu.CompilerParams(
            collective_id=0, has_side_effects=True, vmem_limit_bytes=32 << 20
        ),
    )(
        *(
            pltpu.with_memory_space_constraint(value, pltpu.HBM)
            for value in (
                query[0], dout[0], mem_key[0], mem_value[0], keep_count, keep_slot[0].T, pool_weight[0].T,
            )
        )
    )
    any_space = pl.BlockSpec(memory_space=pl.ANY)
    dq, dk, dv = pl.pallas_call(
        settle_kernel,
        out_shape=(out, out, out),
        in_specs=[any_space] * 3,
        out_specs=(any_space,) * 3,
        scratch_shapes=[dma((3,))],
        compiler_params=pltpu.CompilerParams(vmem_limit_bytes=32 << 20),
    )(dq, dk, dv)
    return dq[None], dk[None], dv[None]


def solution(mesh):
    fused = mesh.shape["seq"] == 16 and mesh.shape["span"] == 2
    return jax.shard_map(
        per_device_fused if fused else per_device,
        mesh=mesh,
        in_specs=(
            P("span", "seq", None),
            P("span", "seq", None),
            P("span", "seq", None),
            P("span", "seq", None),
            P("span", None),
            P("span", "seq", None),
            P("span", "seq", None),
        ),
        out_specs=(P("span", "seq", None), P("span", "seq", None), P("span", "seq", None)),
        check_vma=False,
    )
```
